32 devices in a mesh: seq: 8 (over z, y), tensor: 2 (over x), section: 2 (over core).
Axes of the slice: x: 2, y: 2, z: 4, core: 2. Of those that a mesh axis runs over, the one named last changes fastest.
Arguments:
- encoder_states: bfloat16 [12288, 4096], P(('seq', 'section'), 'tensor'), may hold values from -6 to 6
- key_weight: bfloat16 [4096, 4096], P(None, 'tensor'), may hold values from -0.125 to 0.125
- value_weight: bfloat16 [4096, 4096], P(None, 'tensor'), may hold values from -0.125 to 0.125
- queries: bfloat16 [4096, 4096], P(('seq', 'section'), 'tensor'), may hold values from -400 to 400
- out_grad: bfloat16 [4096, 4096], P(('seq', 'section'), 'tensor'), may hold values from -6 to 6
- band_blocks: int32 [32, 2], P(('seq', 'section')), may hold values from 0 to 95, as said below
Outputs:
- query_grad: bfloat16 [4096, 4096], P(('seq', 'section'), 'tensor')
- encoder_grad: bfloat16 [12288, 4096], P(('seq', 'section'), 'tensor')
The draws below stay inside these ranges and needn't reach their ends.
Inputs may be any that keep to these rules, and one draw needn't show every extreme that they name: band_blocks[b] holds the first and the last encoder block (inclusive, blocks of 128 frames) that decoder block b attends to; both rise with b; the first lies in 3 * b - 2 to 3 * b - 1 and the last in 3 * b + 3 to 3 * b + 4, each clipped to the encoder's blocks; some band spans exactly 7 encoder blocks.
All inputs are finite; a program needn't handle non-finite values.
Results may differ from the reference program's by a relative error of at most 0.006.
The reference program's roundings to bfloat16 on the way (of `keys`, `values`, `probability_low`, `score_grad`, `key_grad`, `value_grad` and `group_term`) count: a program that leaves them out, or rounds other values in their place, can miss the bound.
Values may be sent and summed in bfloat16 or wider, within the bound.
No kernel may reach another device: no remote copies, remote signals or barrier semaphores. Data moves between devices by JAX's collectives and lax.ppermute only.
A program may use at most 192 MiB of HBM per device.

```python
import jax
import jax.numpy as jnp
from jax import lax

D = 4096
H = 32
DH = 128
BLOCK = 128
RATIO = 3
HALO_BLK = 2
TOKENS = 4096
FRAMES = 12288
BAND_MAX = 7
N_TENSOR = 2


def draw_queries(key, part):
    base_values = jnp.clip(jax.random.normal(key, (TOKENS, H * DH), jnp.float32), -5.0, 5.0)
    return base_values.astype(jnp.bfloat16)


def draw_out_grad(key, part):
    base_values = jnp.clip(jax.random.normal(jax.random.fold_in(key, 21), (TOKENS, H * DH), jnp.float32), -6.0, 6.0)
    return base_values.astype(jnp.bfloat16)


def draw_band_blocks(key, part):
    block_count = TOKENS // BLOCK
    enc_blocks = FRAMES // BLOCK
    block_index = jnp.arange(block_count, dtype=jnp.int32)
    before = jax.random.randint(jax.random.fold_in(key, 1), (block_count,), 1, HALO_BLK + 1)
    after = jax.random.randint(jax.random.fold_in(key, 2), (block_count,), 1, HALO_BLK + 1)
    before = jnp.where(block_index == 1, HALO_BLK, before)
    after = jnp.where(block_index == 1, HALO_BLK, after)
    first_block = jnp.clip(RATIO * block_index - before, 0, enc_blocks - 1)
    last_block = jnp.clip(RATIO * block_index + RATIO - 1 + after, 0, enc_blocks - 1)
    return jnp.stack([first_block, last_block], axis=1).astype(jnp.int32)


def with_spikes(entries, own_key, source, target, shards_of, factor):
    owner, partner = [(jnp.arange(entries.shape[dim]) // (entries.shape[dim] // shards_of)).reshape([-1 if axis == dim else 1 for axis in range(entries.ndim)]) for dim in (source, target)]
    chosen = jax.random.permutation(own_key, shards_of)[partner]
    strong = (owner == chosen) | (owner == (partner + shards_of // 2) % shards_of)
    return jnp.where(strong, factor * entries, entries)


def block_scale(stream_key, shape, split, least, high):
    def one(axis_at, blocks):
        draws = jax.random.uniform(jax.random.fold_in(jax.random.fold_in(stream_key, 6), axis_at), (blocks,), jnp.float32, least / len(split), high / len(split))
        return jnp.repeat(jnp.exp(draws), shape[axis_at] // blocks).reshape((-1,) + (1,) * (len(shape) - axis_at - 1))

    gain = one(*split[0])
    for cut in split[1:]:
        gain = gain * one(*cut)
    return gain


def gaussian(rng, dims, width, limit, cuts=(), held_as=jnp.bfloat16):
    result = width * jax.random.normal(rng, dims, jnp.float32)
    if cuts:
        result = result * block_scale(rng, dims, cuts, -0.22, 0.18)
    return jnp.clip(result, -limit, limit).astype(held_as)


def heavy_noise(stream_key, dims, width, bound, pieces, heavy, kind=jnp.bfloat16):
    array = width * jax.random.normal(stream_key, dims, jnp.float32)
    if pieces:
        array = array * block_scale(stream_key, dims, pieces, -0.22, 0.18)
    return jnp.clip(with_spikes(array, jax.random.fold_in(stream_key, 3), *heavy), -bound, bound).astype(kind)


def setup_inputs(seed: int = 0) -> dict:
    key_list = jax.random.split(jax.random.key(seed), 7)
    return {
        "encoder_states": gaussian(key_list[0], (FRAMES, D), 1.0, 6.0, ((0, 16), (1, 2))),
        "key_weight": heavy_noise(key_list[1], (D, H * DH), D ** -0.5, 0.125, ((1, 2),), (1, 0, 2, 2.0)),
        "value_weight": heavy_noise(key_list[2], (D, H * DH), D ** -0.5, 0.125, ((1, 2),), (1, 0, 2, 2.0)),
        "queries": draw_queries(jax.random.fold_in(key_list[6], 71), 0),
        "out_grad": draw_out_grad(jax.random.fold_in(key_list[6], 71), 0),
        "band_blocks": draw_band_blocks(jax.random.fold_in(key_list[6], 71), 0),
    }


def attend(query_rows, grad_rows, key_rows, value_rows, allowed, softmax_scale):
    scores = jnp.einsum('qhd,khd->hqk', query_rows, key_rows) * softmax_scale
    row_max = jnp.max(jnp.where(allowed[None], scores, -jnp.inf), axis=-1, keepdims=True)
    unnormed = jnp.where(allowed[None], jnp.exp(jnp.where(allowed[None], scores, row_max) - row_max), 0.0)
    probability = unnormed / jnp.sum(unnormed, axis=-1, keepdims=True)
    probability_low = probability.astype(jnp.bfloat16)
    attended = jnp.einsum('hqk,khd->qhd', probability_low.astype(jnp.float32), value_rows)
    row_delta = jnp.sum(grad_rows * attended, axis=-1)
    prob_grad = jnp.einsum('qhd,khd->hqk', grad_rows, value_rows)
    score_grad = (probability * (prob_grad - jnp.transpose(row_delta)[:, :, None]) * softmax_scale).astype(jnp.bfloat16)
    query_grad = jnp.einsum('hqk,khd->qhd', score_grad.astype(jnp.float32), key_rows).astype(jnp.bfloat16)
    key_part = jnp.einsum('hqk,qhd->khd', score_grad.astype(jnp.float32), query_rows)
    value_part = jnp.einsum('hqk,qhd->khd', probability_low.astype(jnp.float32), grad_rows)
    return query_grad, key_part, value_part


def reference(encoder_states, key_weight, value_weight, queries, out_grad, band_blocks):
    keys = jnp.dot(encoder_states, key_weight, preferred_element_type=jnp.float32).astype(jnp.bfloat16)
    values = jnp.dot(encoder_states, value_weight, preferred_element_type=jnp.float32).astype(jnp.bfloat16)
    keys_wide = keys.astype(jnp.float32)
    values_wide = values.astype(jnp.float32)
    softmax_scale = DH ** -0.5
    window_len = BAND_MAX * BLOCK
    enc_blocks = FRAMES // BLOCK
    columns = H * DH

    def block_step(carry, block_index):
        key_accum, value_accum = carry
        first_block = band_blocks[block_index, 0]
        last_block = band_blocks[block_index, 1]
        window_base = (jnp.minimum(first_block, enc_blocks - BAND_MAX) * BLOCK).astype(jnp.int32)
        key_rows = lax.dynamic_slice_in_dim(keys_wide, window_base, window_len, 0).reshape(window_len, H, DH)
        value_rows = lax.dynamic_slice_in_dim(values_wide, window_base, window_len, 0).reshape(window_len, H, DH)
        row_start = (block_index * BLOCK).astype(jnp.int32)
        query_rows = lax.dynamic_slice_in_dim(queries, row_start, BLOCK, 0).astype(jnp.float32).reshape(BLOCK, H, DH)
        grad_rows = lax.dynamic_slice_in_dim(out_grad, row_start, BLOCK, 0).astype(jnp.float32).reshape(BLOCK, H, DH)
        position = window_base + jnp.arange(window_len, dtype=jnp.int32)
        in_band = (position >= first_block * BLOCK) & (position < (last_block + 1) * BLOCK)
        allowed = jnp.broadcast_to(in_band[None, :], (BLOCK, window_len))
        query_grad, key_part, value_part = attend(query_rows, grad_rows, key_rows, value_rows, allowed, softmax_scale)
        key_accum = lax.dynamic_update_slice_in_dim(key_accum, lax.dynamic_slice_in_dim(key_accum, window_base, window_len, 0) + key_part.reshape(window_len, columns), window_base, 0)
        value_accum = lax.dynamic_update_slice_in_dim(value_accum, lax.dynamic_slice_in_dim(value_accum, window_base, window_len, 0) + value_part.reshape(window_len, columns), window_base, 0)
        return (key_accum, value_accum), query_grad.reshape(BLOCK, columns)

    zeros_accum = jnp.zeros((FRAMES, columns), jnp.float32)
    (key_accum, value_accum), query_blocks = lax.scan(block_step, (zeros_accum, zeros_accum), jnp.arange(TOKENS // BLOCK, dtype=jnp.int32))
    query_grad = query_blocks.reshape(TOKENS, columns)
    key_grad = key_accum.astype(jnp.bfloat16)
    value_grad = value_accum.astype(jnp.bfloat16)
    groups = N_TENSOR
    group_width = columns // groups
    contract = (((1,), (1,)), ((), ()))

    def group_step(running, group_index):
        col_start = (group_index * group_width).astype(jnp.int32)
        key_piece = lax.dynamic_slice_in_dim(key_grad, col_start, group_width, 1)
        value_piece = lax.dynamic_slice_in_dim(value_grad, col_start, group_width, 1)
        key_cols = lax.dynamic_slice_in_dim(key_weight, col_start, group_width, 1)
        value_cols = lax.dynamic_slice_in_dim(value_weight, col_start, group_width, 1)
        group_term = lax.dot_general(key_piece, key_cols, contract, preferred_element_type=jnp.float32)
        group_term = group_term + lax.dot_general(value_piece, value_cols, contract, preferred_element_type=jnp.float32)
        rounded = lax.optimization_barrier(group_term.astype(jnp.bfloat16)).astype(jnp.float32)
        return running + rounded, None

    running, unused = lax.scan(group_step, jnp.zeros((FRAMES, D), jnp.float32), jnp.arange(groups, dtype=jnp.int32))
    encoder_grad = running.astype(jnp.bfloat16)
    return query_grad, encoder_grad
```

```python
import functools

import jax
import jax.numpy as jnp
from jax import lax
from jax.experimental import pallas as pl
from jax.experimental.pallas import tpu as pltpu
from jax.sharding import PartitionSpec as P

DH = 128
BLOCK = 128
RATIO = 3
HALO_BLK = 2
NEG = -1e30
ROWS = ("seq", "section")
NT = (((1,), (1,)), ((), ()))
TN = (((0,), (0,)), ((), ()))
F32 = jnp.float32
BF16 = jnp.bfloat16


def call(body, grid, scalars, in_specs, out_specs, out_shape, flops, moved, aliases=None, name=None):
    return pl.pallas_call(
        body,
        grid_spec=pltpu.PrefetchScalarGridSpec(
            num_scalar_prefetch=scalars, grid=grid, in_specs=in_specs, out_specs=out_specs
        ),
        out_shape=out_shape,
        input_output_aliases=aliases or {},
        cost_estimate=pl.CostEstimate(flops=flops, bytes_accessed=moved, transcendentals=0),
        name=name,
    )


def project_own(index, states, key_weight, value_weight, cuts):
    rows, depth = states.shape
    columns = key_weight.shape[1]
    wide = min(256, columns)

    def body(index_ref, states_ref, key_ref, value_ref, *outs):
        for at, weight_ref in enumerate((key_ref, value_ref)):
            product = jnp.dot(states_ref[...], weight_ref[...], preferred_element_type=F32)
            for piece, (first, last) in enumerate(cuts):
                outs[2 * piece + at][...] = product[first:last]

    weight_spec = pl.BlockSpec((depth, wide), lambda j, index_ref: (index_ref[0], j))
    shapes, specs = [], []
    for first, last in cuts:
        for _ in range(2):
            shapes.append(jax.ShapeDtypeStruct((last - first, columns), F32))
            specs.append(pl.BlockSpec((last - first, wide), lambda j, index_ref: (0, j)))
    out = call(
        body,
        (columns // wide,),
        1,
        [pl.BlockSpec((rows, depth), lambda j, index_ref: (0, 0)), weight_spec, weight_spec],
        specs,
        shapes,
        4 * rows * depth * columns,
        2 * rows * depth + 4 * depth * columns + 8 * rows * columns,
        name="project_own",
    )(index, states, key_weight, value_weight)
    return [(out[2 * i], out[2 * i + 1]) for i in range(len(cuts))]


def project_rest(index, partial, arrived, key_weight, value_weight):
    rows, columns = partial[0].shape
    depth = arrived[0].shape[1]
    count = len(arrived)
    wide = min(256, columns)

    def body(index_ref, *refs):
        key_part, value_part = refs[:2]
        pieces = refs[2 : 2 + count]
        weights = (refs[2 + count : 2 + 2 * count], refs[2 + 2 * count : 2 + 3 * count])
        outs = refs[2 + 3 * count :]
        for part_ref, weight_refs, out_ref in zip((key_part, value_part), weights, outs):
            total = part_ref[...]
            for piece_ref, weight_ref in zip(pieces, weight_refs):
                total = total + jnp.dot(piece_ref[...], weight_ref[...], preferred_element_type=F32)
            out_ref[...] = total.astype(BF16)

    tile = pl.BlockSpec((rows, wide), lambda j, index_ref: (0, j))
    piece_spec = pl.BlockSpec((rows, depth), lambda j, index_ref: (0, 0))
    weight_specs = [
        pl.BlockSpec((depth, wide), lambda j, index_ref, k=k: (index_ref[k + 1], j))
        for k in range(count)
    ]
    return call(
        body,
        (columns // wide,),
        1,
        [tile, tile] + [piece_spec] * count + weight_specs * 2,
        [tile, tile],
        [jax.ShapeDtypeStruct((rows, columns), BF16)] * 2,
        4 * rows * depth * columns * count,
        count * (2 * rows * depth + 4 * depth * columns) + 12 * rows * columns,
        name="project_rest",
    )(index, *partial, *arrived, *([key_weight] * count), *([value_weight] * count))


def certain(token, frame):
    return RATIO * token - 1 <= frame <= RATIO * token + RATIO


def reaches(token, frame):
    return RATIO * token - HALO_BLK <= frame <= RATIO * token + RATIO - 1 + HALO_BLK


class Tiles:
    def __init__(self, tokens, first, last, halo):
        self.first, self.last, self.tokens = first, last, tokens
        low, high = (-1, tokens + 1) if halo else (0, tokens)
        touched = [
            t for t in range(low, high) if any(reaches(t, f) for f in range(first, last))
        ]
        whole = [t for t in touched if all(reaches(t, f) for f in range(first, last))]
        self.groups = []
        if whole:
            self.groups.append((whole, first, last))
        for t in touched:
            if t not in whole:
                frames = [f for f in range(first, last) if reaches(t, f)]
                self.groups.append(([t], frames[0], frames[-1] + 1))
        self.touched = touched


def token_rows(refs, tokens, own_count, lanes):
    below, own, above = refs
    pieces = []
    for t in tokens:
        if t < 0:
            pieces.append(below[:, lanes])
        elif t >= own_count:
            pieces.append(above[:, lanes])
        else:
            pieces.append(own[t * BLOCK : (t + 1) * BLOCK, lanes])
    return pieces[0] if len(pieces) == 1 else jnp.concatenate(pieces, axis=0)


def tile_allowed(band_ref, token, frame, own_count):
    if 0 <= token < own_count and certain(token, frame):
        return None
    return (band_ref[2 * (token + 1)] <= frame) & (frame <= band_ref[2 * (token + 1) + 1])


def head_tiles(band_ref, tiles, own_count, key_ref, value_ref, query_refs, grad_refs, lanes, scale):
    for tokens, first, last in tiles.groups:
        rows = slice((first - tiles.first) * BLOCK, (last - tiles.first) * BLOCK)
        keys, values = key_ref[rows, lanes], value_ref[rows, lanes]
        query_rows = token_rows(query_refs, tokens, own_count, lanes)
        grad_rows = token_rows(grad_refs, tokens, own_count, lanes)
        scores = lax.dot_general(keys, query_rows, NT, preferred_element_type=F32) * scale
        slopes = lax.dot_general(values, grad_rows, NT, preferred_element_type=F32)
        yield tokens, first, last, keys, query_rows, grad_rows, scores, slopes


def piece(array, frame, position):
    return array[frame * BLOCK : (frame + 1) * BLOCK, position * BLOCK : (position + 1) * BLOCK]


def fold(stats):
    tops = [jnp.where(total > 0, top, NEG) for top, total, _ in stats]
    top = functools.reduce(jnp.maximum, tops)
    gains = [jnp.exp(t - top) for t in tops]
    total = sum(g * s[1] for g, s in zip(gains, stats))
    weighted = sum(g * s[2] for g, s in zip(gains, stats))
    return top, total, weighted


def tile_stats(band_ref, tiles_list, own_count, kv_refs, query_refs, grad_refs, lanes, scale):
    found = {}
    for tiles, (key_ref, value_ref) in zip(tiles_list, kv_refs):
        for tokens, first, last, _, _, _, scores, slopes in head_tiles(
            band_ref, tiles, own_count, key_ref, value_ref, query_refs, grad_refs, lanes, scale
        ):
            for position, t in enumerate(tokens):
                for f in range(first, last):
                    allowed = tile_allowed(band_ref, t, f, own_count)
                    found.setdefault(t, []).append(
                        (allowed, piece(scores, f - first, position), piece(slopes, f - first, position))
                    )
    stats = {}
    for t, entries in found.items():
        shown = [s if a is None else jnp.where(a, s, NEG) for a, s, _ in entries]
        top = jnp.max(functools.reduce(jnp.maximum, shown), axis=0, keepdims=True)
        total = weighted = None
        for (allowed, _, slope), s in zip(entries, shown):
            e = jnp.exp(s - top)
            if allowed is not None:
                e = jnp.where(allowed, e, 0.0)
            total = e if total is None else total + e
            weighted = e * slope if weighted is None else weighted + e * slope
        stats[t] = (
            top,
            jnp.sum(total, axis=0, keepdims=True),
            jnp.sum(weighted, axis=0, keepdims=True),
        )
    return stats


def read_stats(ref, head, row):
    return tuple(ref[head, row + i : row + i + 1, :] for i in range(3))


def write_stats(ref, head, row, stats):
    for i, value in enumerate(stats):
        ref[head, row + i : row + i + 1, :] = value


def token_specs(own_count, wide, head_blocks):
    halo_q = pl.BlockSpec((BLOCK, wide), lambda h, band_ref: (0, h))
    halo_g = pl.BlockSpec((BLOCK, wide), lambda h, band_ref: (0, h + head_blocks))
    own = pl.BlockSpec((own_count * BLOCK, wide), lambda h, band_ref: (0, h))
    return [halo_q, own, halo_q, halo_g, own, halo_g]


def row_stats(band, tiles_list, kvs, queries, grads, below, above, earlier, scale):
    own_count = queries.shape[0] // BLOCK
    columns = queries.shape[1]
    heads = columns // DH
    per = min(2, heads)
    wide = per * DH
    depth = -(-3 * (own_count + 2) // 8) * 8
    count = len(kvs)

    def body(band_ref, *refs):
        tokens = refs[:6]
        kv_refs = [refs[6 + 2 * i : 8 + 2 * i] for i in range(count)]
        rest = refs[6 + 2 * count :]
        out_ref = rest[-1]
        for head in range(per):
            lanes = slice(head * DH, (head + 1) * DH)
            stats = tile_stats(
                band_ref, tiles_list, own_count, kv_refs, tokens[:3], tokens[3:], lanes, scale
            )
            for t in range(-1, own_count + 1):
                row = 3 * (t + 1)
                mine = [stats[t]] if t in stats else []
                if earlier is not None:
                    mine.append(read_stats(rest[0], head, row))
                if len(mine) == 2:
                    mine = [fold(mine)]
                write_stats(out_ref, head, row, mine[0])
            if depth > 3 * (own_count + 2):
                out_ref[head, 3 * (own_count + 2) :, :] = jnp.zeros(
                    (depth - 3 * (own_count + 2), BLOCK), F32
                )

    kv_specs = []
    for key_rows, _ in kvs:
        kv_specs += [pl.BlockSpec((key_rows.shape[0], wide), lambda h, band_ref: (0, h))] * 2
    stat_spec = pl.BlockSpec((per, depth, BLOCK), lambda h, band_ref: (h, 0, 0))
    frames = sum(kv[0].shape[0] for kv in kvs)
    flat = [array for kv in kvs for array in kv]
    extra = [] if earlier is None else [earlier]
    return call(
        body,
        (heads // per,),
        1,
        token_specs(own_count, wide, heads // per) + kv_specs + [stat_spec] * len(extra),
        stat_spec,
        jax.ShapeDtypeStruct((heads, depth, BLOCK), F32),
        8 * frames * 2 * BLOCK * columns,
        4 * frames * columns + 8 * queries.size,
        name="row_stats",
    )(band, below, queries, above, below, grads, above, *flat, *extra)


def gradients(band, tiles, kv, queries, grads, below, above, stats, from_below, from_above, scale):
    own_count = queries.shape[0] // BLOCK
    columns = queries.shape[1]
    heads = columns // DH
    per = min(2, heads)
    wide = per * DH
    frames = kv[0].shape[0]
    touched = tiles.touched
    own_touched = [t for t in touched if 0 <= t < own_count]
    halo_touched = [t for t in touched if t not in own_touched]

    def body(band_ref, *refs):
        tokens = refs[:6]
        key_ref, value_ref = refs[6:8]
        stat_ref, lower_ref, upper_ref = refs[8:11]
        key_out, value_out, own_out = refs[11:14]
        halo_outs = refs[14:]
        for head in range(per):
            lanes = slice(head * DH, (head + 1) * DH)
            rows = {}
            for t in touched:
                parts = [read_stats(stat_ref, head, 3 * (t + 1))]
                if t <= 0:
                    parts.append(read_stats(lower_ref, head, 3 * (own_count + t + 1)))
                if t >= own_count - 1:
                    parts.append(read_stats(upper_ref, head, 3 * (t - own_count + 1)))
                top, total, weighted = fold(parts)
                inverse = 1.0 / total
                rows[t] = (top, inverse, weighted * inverse)
            key_sum = [None] * (tiles.last - tiles.first)
            value_sum = [None] * (tiles.last - tiles.first)
            query_sum = {}
            for group, first, last, keys, query_rows, grad_rows, scores, slopes in head_tiles(
                band_ref, tiles, own_count, key_ref, value_ref, tokens[:3], tokens[3:], lanes, scale
            ):
                low, slope_low = [], []
                for f in range(first, last):
                    low_row, slope_row = [], []
                    for position, t in enumerate(group):
                        top, inverse, delta = rows[t]
                        p = jnp.exp(piece(scores, f - first, position) - top) * inverse
                        d = p * (piece(slopes, f - first, position) - delta) * scale
                        allowed = tile_allowed(band_ref, t, f, own_count)
                        if allowed is not None:
                            p = jnp.where(allowed, p, 0.0)
                            d = jnp.where(allowed, d, 0.0)
                        low_row.append(p.astype(BF16))
                        slope_row.append(d.astype(BF16))
                    low.append(jnp.concatenate(low_row, axis=1))
                    slope_low.append(jnp.concatenate(slope_row, axis=1))
                low = jnp.concatenate(low, axis=0)
                slope_low = jnp.concatenate(slope_low, axis=0)
                key_part = jnp.dot(slope_low, query_rows, preferred_element_type=F32)
                value_part = jnp.dot(low, grad_rows, preferred_element_type=F32)
                query_part = lax.dot_general(slope_low, keys, TN, preferred_element_type=F32)
                for f in range(first, last):
                    at, cut = f - tiles.first, slice((f - first) * BLOCK, (f - first + 1) * BLOCK)
                    key_sum[at] = (
                        key_part[cut] if key_sum[at] is None else key_sum[at] + key_part[cut]
                    )
                    value_sum[at] = (
                        value_part[cut] if value_sum[at] is None else value_sum[at] + value_part[cut]
                    )
                for position, t in enumerate(group):
                    query_sum[t] = query_part[position * BLOCK : (position + 1) * BLOCK]
            for at in range(tiles.last - tiles.first):
                cut = slice(at * BLOCK, (at + 1) * BLOCK)
                key_out[cut, lanes] = key_sum[at].astype(BF16)
                value_out[cut, lanes] = value_sum[at].astype(BF16)
            for at, t in enumerate(own_touched):
                own_out[at * BLOCK : (at + 1) * BLOCK, lanes] = query_sum[t]
            for out_ref, t in zip(halo_outs, halo_touched):
                out_ref[:, lanes] = query_sum[t]

    depth = stats.shape[1]
    stat_spec = pl.BlockSpec((per, depth, BLOCK), lambda h, band_ref: (h, 0, 0))
    kv_spec = pl.BlockSpec((frames, wide), lambda h, band_ref: (0, h))
    own_rows = len(own_touched) * BLOCK
    own_spec = pl.BlockSpec((own_rows, wide), lambda h, band_ref: (0, h))
    halo_spec = pl.BlockSpec((BLOCK, wide), lambda h, band_ref: (0, h))
    out = call(
        body,
        (heads // per,),
        1,
        token_specs(own_count, wide, heads // per) + [kv_spec] * 2 + [stat_spec] * 3,
        [kv_spec, kv_spec, own_spec] + [halo_spec] * len(halo_touched),
        [jax.ShapeDtypeStruct((frames, columns), BF16)] * 2
        + [jax.ShapeDtypeStruct((own_rows, columns), F32)]
        + [jax.ShapeDtypeStruct((BLOCK, columns), F32)] * len(halo_touched),
        20 * frames * 2 * BLOCK * columns,
        8 * frames * columns + 8 * queries.size + 4 * own_rows * columns,
        name="gradients",
    )(band, below, queries, above, below, grads, above, *kv, stats, from_below, from_above)
    return out[:2], (own_touched, out[2]), dict(zip(halo_touched, out[3:]))


def output_terms(index, slot, pieces, key_weight, value_weight, name):
    rows = sum(kg.shape[0] for kg, _ in pieces)
    columns = key_weight.shape[1]
    features = key_weight.shape[0] // lax.axis_size("tensor")
    tall = min(256, features)
    steps = features // tall
    count = len(pieces)

    def body(index_ref, *refs):
        key_ref, value_ref = refs[2 * count : 2 * count + 2]
        out_ref = refs[-1]
        at = 0
        for i in range(count):
            term = lax.dot_general(refs[2 * i][...], key_ref[...], NT, preferred_element_type=F32)
            term = term + lax.dot_general(
                refs[2 * i + 1][...], value_ref[...], NT, preferred_element_type=F32
            )
            size = term.shape[0]
            out_ref[at : at + size, :] = term.astype(BF16)
            at += size

    specs = []
    for kg, _ in pieces:
        specs += [pl.BlockSpec(kg.shape, lambda j, index_ref: (0, 0))] * 2
    weight_spec = pl.BlockSpec((tall, columns), lambda j, index_ref: (index_ref[slot] * steps + j, 0))
    return call(
        body,
        (steps,),
        1,
        specs + [weight_spec] * 2,
        pl.BlockSpec((rows, tall), lambda j, index_ref: (0, j)),
        jax.ShapeDtypeStruct((rows, features), BF16),
        4 * rows * columns * features,
        4 * rows * columns + 4 * columns * features + 2 * rows * features,
        name=name,
    )(index, *[a for pair in pieces for a in pair], key_weight, value_weight)


def add_rows(total, arrived, first):
    rows, features = arrived[0].shape
    tall = BLOCK
    count = len(arrived)

    def body(total_ref, *refs):
        value = total_ref[...].astype(F32)
        for ref in refs[:count]:
            value = value + ref[...].astype(F32)
        refs[count][...] = value.astype(BF16)

    here = pl.BlockSpec((tall, features), lambda i: (i + first // tall, 0))
    return call(
        body,
        (rows // tall,),
        0,
        [here] + [pl.BlockSpec((tall, features), lambda i: (i, 0))] * count,
        here,
        jax.ShapeDtypeStruct(total.shape, total.dtype),
        rows * features * count,
        2 * rows * features * (count + 2),
        aliases={0: 0},
        name="add_rows",
    )(total, *arrived)


def shifted(value, steps):
    count = lax.axis_size(ROWS)
    first, last = (max(0, -steps), min(count, count - steps))
    return lax.ppermute(value, ROWS, [(source, source + steps) for source in range(first, last)])


def on_device(encoder_states, key_weight, value_weight, queries, out_grad, band_blocks):
    frames = encoder_states.shape[0]
    tokens = queries.shape[0]
    own_count = tokens // BLOCK
    frame_blocks = frames // BLOCK
    scale = DH ** (-0.5)
    group = lax.axis_size("tensor")
    me = lax.axis_index("tensor")
    place, places = lax.axis_index(ROWS), lax.axis_size(ROWS)
    edge = HALO_BLK
    cuts = [(0, edge), (frame_blocks - edge, frame_blocks), (edge, frame_blocks - edge)]
    row_cuts = [(first * BLOCK, last * BLOCK) for first, last in cuts]
    turns = [[(i, (i + k) % group) for i in range(group)] for k in range(1, group)]
    sources = jnp.stack([lax.rem(me - k + group, group) for k in range(group)]).astype(jnp.int32)
    targets = jnp.stack([lax.rem(me + k, group) for k in range(group)]).astype(jnp.int32)

    arrived = []
    for first, last in row_cuts:
        rows = encoder_states[first:last]
        arrived.append([lax.ppermute(rows, "tensor", turn) for turn in turns])

    both = jnp.concatenate([queries, out_grad], axis=1)
    below = shifted(both[tokens - BLOCK :], 1)
    above = shifted(both[:BLOCK], -1)
    band_below = shifted(band_blocks[own_count - 1 :], 1)
    band_above = shifted(band_blocks[:1], -1)
    base = place * frame_blocks
    nowhere = jnp.array([[1, 0]], jnp.int32)
    band = jnp.concatenate(
        [
            jnp.where(place > 0, band_below - base, nowhere),
            band_blocks - base,
            jnp.where(place < places - 1, band_above - base, nowhere),
        ],
        axis=0,
    ).reshape(-1)

    partial = project_own(sources, encoder_states, key_weight, value_weight, row_cuts)
    kvs = [
        project_rest(sources, part, pieces, key_weight, value_weight)
        for part, pieces in zip(partial, arrived)
    ]

    tiles = [Tiles(own_count, first, last, i < 2) for i, (first, last) in enumerate(cuts)]
    shared = (queries, out_grad, below, above)
    edge_stats = row_stats(band, tiles[:2], kvs[:2], *shared, None, scale)
    stats = row_stats(band, tiles[2:], kvs[2:], *shared, edge_stats, scale)
    from_below = shifted(stats, 1)
    from_above = shifted(stats, -1)

    out = [None] * 3
    sent = [None] * 3
    for i in (2, 0, 1):
        out[i] = gradients(
            band, tiles[i], kvs[i], *shared, stats, from_below, from_above, scale
        )
        terms = [
            output_terms(targets, k, [out[i][0]], key_weight, value_weight, "terms_away")
            for k in range(1, group)
        ]
        sent[i] = [lax.ppermute(term, "tensor", turn) for term, turn in zip(terms, turns)]

    back_up = shifted(out[1][2][own_count], 1)
    back_down = shifted(out[0][2][-1], -1)
    blocks = [[] for _ in range(own_count)]
    for _, (touched, part), _ in out:
        for at, t in enumerate(touched):
            blocks[t].append(part[at * BLOCK : (at + 1) * BLOCK])
    blocks[0].append(back_up)
    blocks[-1].append(back_down)
    query_grad = jnp.concatenate([sum(parts).astype(BF16) for parts in blocks], axis=0)

    encoder_grad = output_terms(
        targets, 0, [out[0][0], out[2][0], out[1][0]], key_weight, value_weight, "terms_own"
    )
    for i in (2, 0, 1):
        encoder_grad = add_rows(encoder_grad, sent[i], row_cuts[i][0])
    return (query_grad, encoder_grad)


def solution(mesh):
    return jax.shard_map(
        on_device,
        mesh=mesh,
        in_specs=(
            P(ROWS, "tensor"),
            P(None, "tensor"),
            P(None, "tensor"),
            P(ROWS, "tensor"),
            P(ROWS, "tensor"),
            P(ROWS, None),
        ),
        out_specs=(P(ROWS, "tensor"), P(ROWS, "tensor")),
        check_vma=False,
    )
```

```python
import functools
import math

import jax
import jax.numpy as jnp
from jax import lax
from jax.experimental import pallas as pl
from jax.experimental.pallas import tpu as pltpu
from jax.sharding import PartitionSpec as P

DH = 128
BLOCK = 128
RATIO = 3
HALO_BLK = 2
NEG = -1e30
ROWS = ("seq", "section")
NT = (((1,), (1,)), ((), ()))
TN = (((0,), (0,)), ((), ()))
F32 = jnp.float32
BF16 = jnp.bfloat16


ANYWHERE = pl.BlockSpec(memory_space=pl.ANY)
HERE = pl.BlockSpec(memory_space=pltpu.VMEM)
SCALARS = pl.BlockSpec(memory_space=pltpu.SMEM)


def call(body, in_specs, out_specs, out_shape, scratch, flops, moved, name, aliases=None):
    return pl.pallas_call(
        body,
        in_specs=in_specs,
        out_specs=out_specs,
        out_shape=out_shape,
        scratch_shapes=scratch,
        input_output_aliases=aliases or {},
        compiler_params=pltpu.CompilerParams(vmem_limit_bytes=limit_of(scratch)),
        cost_estimate=pl.CostEstimate(flops=flops, bytes_accessed=moved, transcendentals=0),
        name=name,
    )


def limit_of(scratch):
    held = 0
    for item in scratch:
        if item.dtype in (BF16, F32):
            held += math.prod(item.shape) * jnp.dtype(item.dtype).itemsize
    return held + 8 * 2**20


def lanes_at(step, wide):
    return pl.ds(pl.multiple_of(step * wide, wide), wide)


class Weights:
    def __init__(self, key_weight, value_weight, by_columns, group):
        rows, columns = key_weight.shape
        self.features = rows // group
        self.by_columns = by_columns
        if by_columns:
            self.step = min(256, columns)
            self.steps = columns // self.step
            self.block = (self.features, self.step)
        else:
            self.step = min(256, self.features)
            self.steps = self.features // self.step
            self.block = (self.step, columns)

    def buffer_shape(self, count):
        return (count, 2, self.steps) + self.block

    def scratch(self, count):
        return pltpu.VMEM(self.buffer_shape(count), BF16)

    def semaphores(self, count):
        return pltpu.SemaphoreType.DMA((count, 2, self.steps))

    def copy(self, refs, buffer, sems, owner, at, which, step):
        if self.by_columns:
            first = pl.multiple_of(owner * self.features, self.features)
            source = refs[which].at[pl.ds(first, self.features), lanes_at(step, self.step)]
        else:
            first = pl.multiple_of(owner * self.features + step * self.step, self.step)
            source = refs[which].at[pl.ds(first, self.step), :]
        return pltpu.make_async_copy(
            source, buffer.at[at, which, step], sems.at[at, which, step]
        )

    def start(self, refs, buffer, sems, owners):
        for step in range(self.steps):
            for at, owner in enumerate(owners):
                for which in range(2):
                    self.copy(refs, buffer, sems, owner, at, which, step).start()

    def wait(self, refs, buffer, sems, owners, step):
        for at, owner in enumerate(owners):
            for which in range(2):
                self.copy(refs, buffer, sems, owner, at, which, step).wait()


def sources(group):
    me = lax.axis_index("tensor")
    return [lax.rem(me - k + group, group) for k in range(group)]


def targets(group):
    me = lax.axis_index("tensor")
    return [lax.rem(me + k, group) for k in range(group)]


def project_own(states, queries, grads, key_weight, value_weight, cuts, group):
    rows, depth = states.shape
    columns = key_weight.shape[1]
    tokens = queries.shape[0]
    weights = Weights(key_weight, value_weight, True, group)
    count = len(cuts)

    def body(states_ref, query_ref, grad_ref, key_ref, value_ref, *refs):
        outs = refs[: 2 * count]
        up_ref, down_ref = refs[2 * count : 2 * count + 2]
        buffer, sems = refs[2 * count + 2 :]
        owners = sources(group)[:1]
        both = (key_ref, value_ref)
        weights.start(both, buffer, sems, owners)
        for at, ref in enumerate((query_ref, grad_ref)):
            lanes = slice(at * columns, (at + 1) * columns)
            up_ref[:, lanes] = ref[tokens - BLOCK :, :]
            down_ref[:, lanes] = ref[:BLOCK, :]

        def step(j, carry):
            weights.wait(both, buffer, sems, owners, j)
            for which in range(2):
                product = jnp.dot(
                    states_ref[...], buffer[0, which, j], preferred_element_type=F32
                )
                for piece_at, (first, last) in enumerate(cuts):
                    outs[2 * piece_at + which][:, lanes_at(j, weights.step)] = product[first:last]
            return carry

        lax.fori_loop(0, weights.steps, step, 0)

    shapes = []
    for first, last in cuts:
        shapes += [jax.ShapeDtypeStruct((last - first, columns), F32)] * 2
    edge = jax.ShapeDtypeStruct((BLOCK, 2 * columns), BF16)
    out = call(
        body,
        [HERE] * 3 + [ANYWHERE] * 2,
        [HERE] * (len(shapes) + 2),
        shapes + [edge, edge],
        [weights.scratch(1), weights.semaphores(1)],
        4 * rows * depth * columns,
        2 * rows * depth + 4 * depth * columns,
        "project_own",
    )(states, queries, grads, key_weight, value_weight)
    return [(out[2 * i], out[2 * i + 1]) for i in range(count)], out[-2], out[-1]


def project_rest(partial, arrived, key_weight, value_weight, held, group):
    rows, columns = partial[0].shape
    depth = arrived[0].shape[1]
    count = len(arrived)
    weights = Weights(key_weight, value_weight, True, group)
    loads = held is None

    def body(key_part, value_part, *refs):
        pieces, refs = refs[:count], refs[count:]
        if loads:
            both, outs, (buffer, sems) = refs[:2], refs[2:4], refs[4:]
            owners = sources(group)[1:]
            weights.start(both, buffer, sems, owners)
        else:
            buffer, outs = refs[0], refs[1:]

        def step(j, carry):
            if loads:
                weights.wait(both, buffer, sems, owners, j)
            here = lanes_at(j, weights.step)
            for which, part_ref in enumerate((key_part, value_part)):
                total = part_ref[:, here]
                for at in range(count):
                    total = total + jnp.dot(
                        pieces[at][...], buffer[at, which, j], preferred_element_type=F32
                    )
                outs[which][:, here] = total.astype(BF16)
            return carry

        lax.fori_loop(0, weights.steps, step, 0)

    shapes = [jax.ShapeDtypeStruct((rows, columns), BF16)] * 2
    if loads:
        shapes.append(jax.ShapeDtypeStruct(weights.buffer_shape(count), BF16))
    out = call(
        body,
        [HERE] * (2 + count) + ([ANYWHERE] * 2 if loads else [HERE]),
        [HERE] * len(shapes),
        shapes,
        [weights.semaphores(count)] if loads else [],
        4 * rows * depth * columns * count,
        4 * depth * columns * count if loads else 2 * rows * columns,
        "project_rest",
    )(*partial, *arrived, *((key_weight, value_weight) if loads else (held,)))
    return (out[0], out[1]), (out[2] if loads else held)


def certain(token, frame):
    return RATIO * token - 1 <= frame <= RATIO * token + RATIO


def reaches(token, frame):
    return RATIO * token - HALO_BLK <= frame <= RATIO * token + RATIO - 1 + HALO_BLK


class Tiles:
    def __init__(self, tokens, first, last, halo):
        self.first, self.last, self.tokens = first, last, tokens
        low, high = (-1, tokens + 1) if halo else (0, tokens)
        touched = [
            t for t in range(low, high) if any(reaches(t, f) for f in range(first, last))
        ]
        whole = [t for t in touched if all(reaches(t, f) for f in range(first, last))]
        self.groups = []
        if whole:
            self.groups.append((whole, first, last))
        for t in touched:
            if t not in whole:
                frames = [f for f in range(first, last) if reaches(t, f)]
                self.groups.append(([t], frames[0], frames[-1] + 1))
        self.touched = touched


class Tokens:
    def __init__(self, own_count, columns, refs):
        self.own_count, self.columns = own_count, columns
        self.query_ref, self.grad_ref = refs[:2]
        self.below_ref, self.above_ref = refs[2:] if len(refs) > 2 else (None, None)

    def rows(self, tokens, head, grads):
        own_ref = self.grad_ref if grads else self.query_ref
        lanes = lanes_at(head, DH)
        halo = lanes_at(head + (self.columns // DH if grads else 0), DH)
        pieces = []
        for t in tokens:
            if t < 0:
                pieces.append(self.below_ref[:, halo])
            elif t >= self.own_count:
                pieces.append(self.above_ref[:, halo])
            else:
                pieces.append(own_ref[t * BLOCK : (t + 1) * BLOCK, lanes])
        return pieces[0] if len(pieces) == 1 else jnp.concatenate(pieces, axis=0)


def tile_allowed(band_ref, token, frame, own_count):
    if 0 <= token < own_count and certain(token, frame):
        return None
    return (band_ref[2 * (token + 1)] <= frame) & (frame <= band_ref[2 * (token + 1) + 1])


def head_tiles(tiles, tokens, key_ref, value_ref, head):
    lanes = lanes_at(head, DH)
    for group, first, last in tiles.groups:
        rows = slice((first - tiles.first) * BLOCK, (last - tiles.first) * BLOCK)
        keys, values = key_ref[rows, lanes], value_ref[rows, lanes]
        query_rows = tokens.rows(group, head, False)
        grad_rows = tokens.rows(group, head, True)
        scores = lax.dot_general(keys, query_rows, NT, preferred_element_type=F32)
        slopes = lax.dot_general(values, grad_rows, NT, preferred_element_type=F32)
        yield group, first, last, keys, query_rows, grad_rows, scores, slopes


def piece(array, frame, position):
    return array[frame * BLOCK : (frame + 1) * BLOCK, position * BLOCK : (position + 1) * BLOCK]


def fold(stats, rate):
    tops = [jnp.where(total > 0, top, NEG) for top, total, _ in stats]
    top = functools.reduce(jnp.maximum, tops)
    gains = [jnp.exp2((t - top) * rate) for t in tops]
    total = sum(g * s[1] for g, s in zip(gains, stats))
    weighted = sum(g * s[2] for g, s in zip(gains, stats))
    return top, total, weighted


def tile_stats(band_ref, tiles_list, tokens, kv_refs, head, rate):
    found = {}
    for tiles, (key_ref, value_ref) in zip(tiles_list, kv_refs):
        for group, first, last, _, _, _, scores, slopes in head_tiles(
            tiles, tokens, key_ref, value_ref, head
        ):
            for position, t in enumerate(group):
                for f in range(first, last):
                    allowed = tile_allowed(band_ref, t, f, tokens.own_count)
                    found.setdefault(t, []).append(
                        (allowed, piece(scores, f - first, position), piece(slopes, f - first, position))
                    )
    stats = {}
    for t, entries in found.items():
        shown = [s if a is None else jnp.where(a, s, NEG) for a, s, _ in entries]
        top = jnp.max(functools.reduce(jnp.maximum, shown), axis=0, keepdims=True)
        total = weighted = None
        for (allowed, _, slope), s in zip(entries, shown):
            e = jnp.exp2((s - top) * rate)
            if allowed is not None:
                e = jnp.where(allowed, e, 0.0)
            total = e if total is None else total + e
            weighted = e * slope if weighted is None else weighted + e * slope
        stats[t] = (
            top,
            jnp.sum(total, axis=0, keepdims=True),
            jnp.sum(weighted, axis=0, keepdims=True),
        )
    return stats


def read_stats(ref, head, row):
    return tuple(ref[head, row + i : row + i + 1, :] for i in range(3))


def stat_depth(own_count):
    return -(-3 * (own_count + 2) // 8) * 8


def row_stats(band, tiles_list, kvs, queries, grads, below, above, earlier, rate):
    own_count = queries.shape[0] // BLOCK
    columns = queries.shape[1]
    heads = columns // DH
    per = min(2, heads)
    depth = stat_depth(own_count)
    count = len(kvs)
    halo = any(t < 0 or t >= own_count for tiles in tiles_list for t in tiles.touched)
    shared = (queries, grads) + ((below, above) if halo else ())

    def body(band_ref, *refs):
        tokens = Tokens(own_count, columns, refs[: len(shared)])
        refs = refs[len(shared) :]
        kv_refs = [refs[2 * i : 2 * i + 2] for i in range(count)]
        rest = refs[2 * count :]
        out_ref = rest[-1]

        def step(pair, carry):
            for k in range(per):
                head = pair * per + k
                stats = tile_stats(band_ref, tiles_list, tokens, kv_refs, head, rate)
                for t in range(-1, own_count + 1):
                    row = 3 * (t + 1)
                    mine = [stats[t]] if t in stats else []
                    if earlier is not None:
                        mine.append(read_stats(rest[0], head, row))
                    result = mine[0] if len(mine) == 1 else fold(mine, rate)
                    for i, value in enumerate(result):
                        out_ref[head, row + i : row + i + 1, :] = value
                used = 3 * (own_count + 2)
                if depth > used:
                    out_ref[head, used:, :] = jnp.zeros((depth - used, BLOCK), F32)
            return carry

        lax.fori_loop(0, heads // per, step, 0)

    frames = sum(kv[0].shape[0] for kv in kvs)
    flat = [array for kv in kvs for array in kv]
    extra = [] if earlier is None else [earlier]
    return call(
        body,
        [SCALARS] + [HERE] * (len(shared) + len(flat) + len(extra)),
        HERE,
        jax.ShapeDtypeStruct((heads, depth, BLOCK), F32),
        [],
        8 * frames * 2 * BLOCK * columns,
        4 * frames * columns + 8 * queries.size,
        "row_stats",
    )(band, *shared, *flat, *extra)


def away_terms(weights, both, buffer, sems, owners, gradient_refs, outs):
    def step(j, carry):
        weights.wait(both, buffer, sems, owners, j)
        for at, out_ref in enumerate(outs):
            row = 0
            for key_ref, value_ref in gradient_refs:
                term = lax.dot_general(
                    key_ref[...], buffer[at, 0, j], NT, preferred_element_type=F32
                )
                term = term + lax.dot_general(
                    value_ref[...], buffer[at, 1, j], NT, preferred_element_type=F32
                )
                size = term.shape[0]
                out_ref[row : row + size, lanes_at(j, weights.step)] = term.astype(BF16)
                row += size
        return carry

    lax.fori_loop(0, weights.steps, step, 0)


def gradients(
    band, tiles, kv, queries, grads, below, above, stats, swaps, key_weight, value_weight, rate, scale, group
):
    own_count = queries.shape[0] // BLOCK
    columns = queries.shape[1]
    heads = columns // DH
    per = min(2, heads)
    frames = kv[0].shape[0]
    touched = tiles.touched
    own_touched = [t for t in touched if 0 <= t < own_count]
    halo_touched = [t for t in touched if t not in own_touched]
    shared = (queries, grads) + ((below, above) if halo_touched else ())
    weights = Weights(key_weight, value_weight, False, group)

    def body(band_ref, *refs):
        tokens = Tokens(own_count, columns, refs[: len(shared)])
        refs = refs[len(shared) :]
        key_ref, value_ref, stat_ref, even_ref, odd_ref = refs[:5]
        both, refs = refs[5:7], refs[7:]
        key_out, value_out, own_out = refs[:3]
        term_outs = refs[3 : 2 + group]
        halo_outs = refs[2 + group : -2]
        buffer, sems = refs[-2:]
        owners = targets(group)[1:]
        weights.start(both, buffer, sems, owners)
        even = lax.rem(lax.axis_index(ROWS), 2) == 0

        def one(head):
            rows = {}
            for t in touched:
                parts = [read_stats(stat_ref, head, 3 * (t + 1))]
                if t <= 0:
                    row = 3 * (own_count + t + 1)
                    first, second = read_stats(odd_ref, head, row), read_stats(even_ref, head, row)
                    parts.append([jnp.where(even, a, b) for a, b in zip(first, second)])
                if t >= own_count - 1:
                    row = 3 * (t - own_count + 1)
                    first, second = read_stats(even_ref, head, row), read_stats(odd_ref, head, row)
                    parts.append([jnp.where(even, a, b) for a, b in zip(first, second)])
                top, total, weighted = fold(parts, rate)
                rows[t] = (top * rate + jnp.log2(total), weighted / total)
            key_sum = [None] * (tiles.last - tiles.first)
            value_sum = [None] * (tiles.last - tiles.first)
            query_sum = {}
            for group_tokens, first, last, keys, query_rows, grad_rows, scores, slopes in head_tiles(
                tiles, tokens, key_ref, value_ref, head
            ):
                low, slope_low = [], []
                for f in range(first, last):
                    low_row, slope_row = [], []
                    for position, t in enumerate(group_tokens):
                        level, delta = rows[t]
                        p = jnp.exp2(piece(scores, f - first, position) * rate - level)
                        d = p * (piece(slopes, f - first, position) - delta) * scale
                        allowed = tile_allowed(band_ref, t, f, own_count)
                        if allowed is not None:
                            p = jnp.where(allowed, p, 0.0)
                            d = jnp.where(allowed, d, 0.0)
                        low_row.append(p.astype(BF16))
                        slope_row.append(d.astype(BF16))
                    low.append(jnp.concatenate(low_row, axis=1))
                    slope_low.append(jnp.concatenate(slope_row, axis=1))
                low = jnp.concatenate(low, axis=0)
                slope_low = jnp.concatenate(slope_low, axis=0)
                key_part = jnp.dot(slope_low, query_rows, preferred_element_type=F32)
                value_part = jnp.dot(low, grad_rows, preferred_element_type=F32)
                query_part = lax.dot_general(slope_low, keys, TN, preferred_element_type=F32)
                for f in range(first, last):
                    at, cut = f - tiles.first, slice((f - first) * BLOCK, (f - first + 1) * BLOCK)
                    for sums, part in ((key_sum, key_part), (value_sum, value_part)):
                        sums[at] = part[cut] if sums[at] is None else sums[at] + part[cut]
                for position, t in enumerate(group_tokens):
                    query_sum[t] = query_part[position * BLOCK : (position + 1) * BLOCK]
            lanes = lanes_at(head, DH)
            for at in range(tiles.last - tiles.first):
                cut = slice(at * BLOCK, (at + 1) * BLOCK)
                key_out[cut, lanes] = key_sum[at].astype(BF16)
                value_out[cut, lanes] = value_sum[at].astype(BF16)
            for at, t in enumerate(own_touched):
                own_out[at * BLOCK : (at + 1) * BLOCK, lanes] = query_sum[t]
            for out_ref, t in zip(halo_outs, halo_touched):
                out_ref[:, lanes] = query_sum[t]

        def step(pair, carry):
            for k in range(per):
                one(pair * per + k)
            return carry

        lax.fori_loop(0, heads // per, step, 0)
        away_terms(weights, both, buffer, sems, owners, [(key_out, value_out)], term_outs)

    own_rows = len(own_touched) * BLOCK
    shapes = (
        [jax.ShapeDtypeStruct((frames, columns), BF16)] * 2
        + [jax.ShapeDtypeStruct((own_rows, columns), F32)]
        + [jax.ShapeDtypeStruct((frames, weights.features), BF16)] * (group - 1)
        + [jax.ShapeDtypeStruct((BLOCK, columns), F32)] * len(halo_touched)
    )
    out = call(
        body,
        [SCALARS] + [HERE] * (len(shared) + 5) + [ANYWHERE] * 2,
        [HERE] * len(shapes),
        shapes,
        [weights.scratch(group - 1), weights.semaphores(group - 1)],
        20 * frames * 2 * BLOCK * columns + 4 * frames * columns * weights.features * (group - 1),
        4 * columns * weights.features * (group - 1) + 8 * frames * columns,
        "gradients",
    )(band, *shared, *kv, stats, *swaps, key_weight, value_weight)
    halo = dict(zip(halo_touched, out[2 + group :]))
    return out[:2], (own_touched, out[2]), out[3 : 2 + group], halo


def own_terms(pieces, key_weight, value_weight, group):
    rows = sum(kg.shape[0] for kg, _ in pieces)
    columns = key_weight.shape[1]
    weights = Weights(key_weight, value_weight, False, group)
    count = len(pieces)

    def body(*refs):
        gradient_refs = [refs[2 * i : 2 * i + 2] for i in range(count)]
        both = refs[2 * count : 2 * count + 2]
        out_ref, buffer, sems = refs[2 * count + 2 :]
        owners = targets(group)[:1]
        weights.start(both, buffer, sems, owners)
        away_terms(weights, both, buffer, sems, owners, gradient_refs, [out_ref])

    return call(
        body,
        [HERE] * (2 * count) + [ANYWHERE] * 2,
        HERE,
        jax.ShapeDtypeStruct((rows, weights.features), BF16),
        [weights.scratch(1), weights.semaphores(1)],
        4 * rows * columns * weights.features,
        4 * columns * weights.features,
        "own_terms",
    )(*[a for pair in pieces for a in pair], key_weight, value_weight)


def add_rows(target, own, arrived, first):
    rows, features = arrived[0].shape
    tall = BLOCK // 2
    steps = rows // tall
    count = len(arrived)

    def body(own_ref, *refs):
        terms = refs[:count]
        out_ref, buffer, sems = refs[-3:]
        copies = []
        for i in range(steps):
            value = own_ref[first + i * tall : first + (i + 1) * tall, :].astype(F32)
            for ref in terms:
                value = value + ref[i * tall : (i + 1) * tall, :].astype(F32)
            buffer[i] = value.astype(BF16)
            copy = pltpu.make_async_copy(
                buffer.at[i], out_ref.at[pl.ds(first + i * tall, tall), :], sems.at[i]
            )
            copy.start()
            copies.append(copy)
        for copy in copies:
            copy.wait()

    extra = [] if target is None else [target]
    return call(
        body,
        [HERE] * (1 + count) + [ANYWHERE] * len(extra),
        ANYWHERE,
        jax.ShapeDtypeStruct(own.shape, own.dtype),
        [pltpu.VMEM((steps, tall, features), BF16), pltpu.SemaphoreType.DMA((steps,))],
        rows * features * count,
        2 * rows * features * (count + 2),
        "add_rows",
        {1 + count: 0} if extra else None,
    )(own, *arrived, *extra)


def shifted(value, steps):
    count = lax.axis_size(ROWS)
    first, last = (max(0, -steps), min(count, count - steps))
    return lax.ppermute(value, ROWS, [(source, source + steps) for source in range(first, last)])


def swapped(value, first):
    pairs = []
    for at in range(first, lax.axis_size(ROWS) - 1, 2):
        pairs += [(at, at + 1), (at + 1, at)]
    return lax.ppermute(value, ROWS, pairs)


def on_device(encoder_states, key_weight, value_weight, queries, out_grad, band_blocks):
    frames = encoder_states.shape[0]
    tokens = queries.shape[0]
    own_count = tokens // BLOCK
    frame_blocks = frames // BLOCK
    scale = DH ** (-0.5)
    rate = scale * math.log2(math.e)
    group = lax.axis_size("tensor")
    place, places = lax.axis_index(ROWS), lax.axis_size(ROWS)
    edge = HALO_BLK
    cuts = [(0, edge), (frame_blocks - edge, frame_blocks), (edge, frame_blocks - edge)]
    row_cuts = [(first * BLOCK, last * BLOCK) for first, last in cuts]
    turns = [[(i, (i + k) % group) for i in range(group)] for k in range(1, group)]

    arrived = []
    for first, last in row_cuts:
        rows = encoder_states[first:last]
        arrived.append([lax.ppermute(rows, "tensor", turn) for turn in turns])

    partial, edge_up, edge_down = project_own(
        encoder_states, queries, out_grad, key_weight, value_weight, row_cuts, group
    )
    edge_up, edge_down, band_blocks = lax.optimization_barrier((edge_up, edge_down, band_blocks))
    below = shifted(edge_up, 1)
    above = shifted(edge_down, -1)
    band_below = shifted(band_blocks[own_count - 1 :], 1)
    band_above = shifted(band_blocks[:1], -1)
    base = place * frame_blocks
    nowhere = jnp.array([[1, 0]], jnp.int32)
    band = jnp.concatenate(
        [
            jnp.where(place > 0, band_below - base, nowhere),
            band_blocks - base,
            jnp.where(place < places - 1, band_above - base, nowhere),
        ],
        axis=0,
    ).reshape(-1)

    kvs, held = [], None
    for part, pieces in zip(partial, arrived):
        kv, held = project_rest(part, pieces, key_weight, value_weight, held, group)
        kvs.append(kv)

    tiles = [Tiles(own_count, first, last, i < 2) for i, (first, last) in enumerate(cuts)]
    shared = (queries, out_grad, below, above)
    edge_stats = row_stats(band, tiles[:2], kvs[:2], *shared, None, rate)
    stats = row_stats(band, tiles[2:], kvs[2:], *shared, edge_stats, rate)
    swaps = (swapped(stats, 0), swapped(stats, 1))

    out = [None] * 3
    sent = [None] * 3
    for i in (2, 0, 1):
        out[i] = gradients(
            band, tiles[i], kvs[i], *shared, stats, swaps, key_weight, value_weight, rate, scale, group
        )
        sent[i] = [lax.ppermute(term, "tensor", turn) for term, turn in zip(out[i][2], turns)]

    back_up = shifted(out[1][3][own_count], 1)
    back_down = shifted(out[0][3][-1], -1)
    blocks = [[] for _ in range(own_count)]
    for _, (touched, part), _, _ in out:
        for at, t in enumerate(touched):
            blocks[t].append(part[at * BLOCK : (at + 1) * BLOCK])
    blocks[0].append(back_up)
    blocks[-1].append(back_down)
    query_grad = jnp.concatenate([sum(parts).astype(BF16) for parts in blocks], axis=0)

    own = own_terms([out[0][0], out[2][0], out[1][0]], key_weight, value_weight, group)
    encoder_grad = None
    for i in (2, 0, 1):
        encoder_grad = add_rows(encoder_grad, own, sent[i], row_cuts[i][0])
    return (query_grad, encoder_grad)


def solution(mesh):
    return jax.shard_map(
        on_device,
        mesh=mesh,
        in_specs=(
            P(ROWS, "tensor"),
            P(None, "tensor"),
            P(None, "tensor"),
            P(ROWS, "tensor"),
            P(ROWS, "tensor"),
            P(ROWS, None),
        ),
        out_specs=(P(ROWS, "tensor"), P(ROWS, "tensor")),
        check_vma=False,
    )
```

```python
import functools
import math

import jax
import jax.numpy as jnp
from jax import lax
from jax.experimental import pallas as pl
from jax.experimental.pallas import tpu as pltpu
from jax.sharding import PartitionSpec as P


DH = 128
BLOCK = 128
RATIO = 3
HALO_BLK = 2
NEG = -1e30
WINDOW = 3
PER_STATS = 4
PER_GRADIENTS = 4
ROWS = ("seq", "section")
NT = (((1,), (1,)), ((), ()))
TN = (((0,), (0,)), ((), ()))
F32 = jnp.float32
BF16 = jnp.bfloat16


ANYWHERE = pl.BlockSpec(memory_space=pltpu.HBM)
HERE = pl.BlockSpec(memory_space=pltpu.VMEM)
SCALARS = pl.BlockSpec(memory_space=pltpu.SMEM)


def call(body, in_specs, out_specs, out_shape, scratch, flops, moved, aliases=None):
    return pl.pallas_call(
        body,
        in_specs=in_specs,
        out_specs=out_specs,
        out_shape=out_shape,
        scratch_shapes=scratch,
        input_output_aliases=aliases or {},
        compiler_params=pltpu.CompilerParams(vmem_limit_bytes=limit_of(scratch)),
        cost_estimate=pl.CostEstimate(flops=flops, bytes_accessed=moved, transcendentals=0),
    )


def limit_of(scratch):
    held = 0
    for item in scratch:
        if item.dtype in (BF16, F32):
            held += math.prod(item.shape) * jnp.dtype(item.dtype).itemsize
    return held + 3 * 2**20


def lanes_at(step, wide):
    return pl.ds(pl.multiple_of(step * wide, wide), wide)


class Weights:
    def __init__(self, key_weight, by_columns, group):
        rows, columns = key_weight.shape
        self.features = rows // group
        self.by_columns = by_columns
        if by_columns:
            self.step = min(256, columns)
            self.steps = columns // self.step
            self.block = (self.features, self.step)
        else:
            self.step = min(256, self.features)
            self.steps = self.features // self.step
            self.block = (self.step, columns)

    def buffer_shape(self, count):
        return (count, 2, self.steps) + self.block

    def scratch(self, count):
        return pltpu.VMEM(self.buffer_shape(count), BF16)

    def semaphores(self, count):
        return pltpu.SemaphoreType.DMA((count, 2, self.steps))

    def copy(self, refs, buffer, sems, owner, at, which, step):
        if self.by_columns:
            first = pl.multiple_of(owner * self.features, self.features)
            source = refs[which].at[pl.ds(first, self.features), lanes_at(step, self.step)]
        else:
            first = pl.multiple_of(owner * self.features + step * self.step, self.step)
            source = refs[which].at[pl.ds(first, self.step), :]
        return pltpu.make_async_copy(
            source, buffer.at[at, which, step], sems.at[at, which, step]
        )

    def start_step(self, refs, buffer, sems, owners, step):
        for at, owner in enumerate(owners):
            for which in range(2):
                self.copy(refs, buffer, sems, owner, at, which, step).start()

    def start(self, refs, buffer, sems, owners, window=None):
        for step in range(min(self.steps, window or self.steps)):
            self.start_step(refs, buffer, sems, owners, step)

    def wait(self, refs, buffer, sems, owners, step):
        for at, owner in enumerate(owners):
            for which in range(2):
                self.copy(refs, buffer, sems, owner, at, which, step).wait()

    def advance(self, refs, buffer, sems, owners, step):
        self.wait(refs, buffer, sems, owners, step)

        @pl.when(step + WINDOW < self.steps)
        def _():
            self.start_step(refs, buffer, sems, owners, step + WINDOW)


def sources(group):
    me = lax.axis_index("tensor")
    return [lax.rem(me - k + group, group) for k in range(group)]


def targets(group):
    me = lax.axis_index("tensor")
    return [lax.rem(me + k, group) for k in range(group)]


def take_rows(states, cuts):
    def body(states_ref, *refs):
        outs, sems = refs[:-1], refs[-1]
        copies = []
        for i, (first, last) in enumerate(cuts):
            copies.append(
                pltpu.make_async_copy(states_ref.at[pl.ds(first, last - first), :], outs[i], sems.at[i])
            )
            copies[-1].start()
        for copy in copies:
            copy.wait()

    shapes = [jax.ShapeDtypeStruct((last - first, states.shape[1]), BF16) for first, last in cuts]
    return call(
        body,
        [ANYWHERE],
        [HERE] * len(cuts),
        shapes,
        [pltpu.SemaphoreType.DMA((len(cuts),))],
        0,
        4 * sum(math.prod(shape.shape) for shape in shapes),
    )(pltpu.with_memory_space_constraint(states, pltpu.HBM))


def project_own(states, queries, grads, key_weight, value_weight, cuts, group):
    rows, depth = states.shape
    columns = key_weight.shape[1]
    tokens = queries.shape[0]
    weights = Weights(key_weight, True, group)
    count = len(cuts)

    def body(states_ref, query_ref, grad_ref, key_ref, value_ref, *refs):
        outs = refs[: 2 * count]
        up_ref, down_ref = refs[2 * count : 2 * count + 2]
        buffer, sems = refs[2 * count + 2 :]
        owners = sources(group)[:1]
        both = (key_ref, value_ref)
        weights.start(both, buffer, sems, owners, WINDOW)
        for at, ref in enumerate((query_ref, grad_ref)):
            lanes = slice(at * columns, (at + 1) * columns)
            up_ref[:, lanes] = ref[tokens - BLOCK :, :]
            down_ref[:, lanes] = ref[:BLOCK, :]

        def step(j, carry):
            weights.advance(both, buffer, sems, owners, j)
            for which in range(2):
                product = jnp.dot(
                    states_ref[...], buffer[0, which, j], preferred_element_type=F32
                )
                for piece_at, (first, last) in enumerate(cuts):
                    outs[2 * piece_at + which][:, lanes_at(j, weights.step)] = product[first:last]
            return carry

        lax.fori_loop(0, weights.steps, step, 0)

    shapes = []
    for first, last in cuts:
        shapes += [jax.ShapeDtypeStruct((last - first, columns), F32)] * 2
    edge = jax.ShapeDtypeStruct((BLOCK, 2 * columns), BF16)
    out = call(
        body,
        [HERE] * 3 + [ANYWHERE] * 2,
        [HERE] * (len(shapes) + 2),
        shapes + [edge, edge],
        [weights.scratch(1), weights.semaphores(1)],
        4 * rows * depth * columns,
        2 * rows * depth + 4 * depth * columns,
    )(states, queries, grads, key_weight, value_weight)
    return [(out[2 * i], out[2 * i + 1]) for i in range(count)], out[-2], out[-1]


def project_rest(partial, arrived, key_weight, value_weight, held, group):
    rows, columns = partial[0].shape
    depth = arrived[0].shape[1]
    count = len(arrived)
    weights = Weights(key_weight, True, group)
    loads = held is None

    def body(key_part, value_part, *refs):
        pieces, refs = refs[:count], refs[count:]
        if loads:
            both, outs, (buffer, sems) = refs[:2], refs[2:4], refs[4:]
            owners = sources(group)[1:]
            weights.start(both, buffer, sems, owners, WINDOW)
        else:
            buffer, outs = refs[0], refs[1:]

        def step(j, carry):
            if loads:
                weights.advance(both, buffer, sems, owners, j)
            here = lanes_at(j, weights.step)
            for which, part_ref in enumerate((key_part, value_part)):
                total = part_ref[:, here]
                for at in range(count):
                    total = total + jnp.dot(
                        pieces[at][...], buffer[at, which, j], preferred_element_type=F32
                    )
                outs[which][:, here] = total.astype(BF16)
            return carry

        lax.fori_loop(0, weights.steps, step, 0)

    shapes = [jax.ShapeDtypeStruct((rows, columns), BF16)] * 2
    if loads:
        shapes.append(jax.ShapeDtypeStruct(weights.buffer_shape(count), BF16))
    out = call(
        body,
        [HERE] * (2 + count) + ([ANYWHERE] * 2 if loads else [HERE]),
        [HERE] * len(shapes),
        shapes,
        [weights.semaphores(count)] if loads else [],
        4 * rows * depth * columns * count,
        4 * depth * columns * count if loads else 2 * rows * columns,
    )(*partial, *arrived, *((key_weight, value_weight) if loads else (held,)))
    return (out[0], out[1]), (out[2] if loads else held)


def certain(token, frame):
    return RATIO * token - 1 <= frame <= RATIO * token + RATIO


def reaches(token, frame):
    return RATIO * token - HALO_BLK <= frame <= RATIO * token + RATIO - 1 + HALO_BLK


class Tiles:
    def __init__(self, tokens, first, last, halo):
        self.first, self.last, self.tokens = first, last, tokens
        low, high = (-1, tokens + 1) if halo else (0, tokens)
        touched = [
            t for t in range(low, high) if any(reaches(t, f) for f in range(first, last))
        ]
        whole = [t for t in touched if all(reaches(t, f) for f in range(first, last))]
        self.groups = []
        if whole:
            self.groups.append((whole, first, last))
        for t in touched:
            if t not in whole:
                frames = [f for f in range(first, last) if reaches(t, f)]
                self.groups.append(([t], frames[0], frames[-1] + 1))
        self.touched = touched


class Tokens:
    def __init__(self, own_count, columns, refs):
        self.own_count, self.columns = own_count, columns
        self.query_ref, self.grad_ref = refs[:2]
        self.below_ref, self.above_ref = refs[2:] if len(refs) > 2 else (None, None)

    def rows(self, tokens, head, grads):
        own_ref = self.grad_ref if grads else self.query_ref
        lanes = lanes_at(head, DH)
        halo = lanes_at(head + (self.columns // DH if grads else 0), DH)
        pieces = []
        for t in tokens:
            if t < 0:
                pieces.append(self.below_ref[:, halo])
            elif t >= self.own_count:
                pieces.append(self.above_ref[:, halo])
            else:
                pieces.append(own_ref[t * BLOCK : (t + 1) * BLOCK, lanes])
        return pieces[0] if len(pieces) == 1 else jnp.concatenate(pieces, axis=0)


class Bands:
    def __init__(self, refs, own_count):
        self.below_ref, self.own_ref, self.above_ref = refs
        self.own_count = own_count
        self.place, self.places = lax.axis_index(ROWS), lax.axis_size(ROWS)

    def allowed(self, token, frame):
        inside = None
        if token < 0:
            ref, row = self.below_ref, self.own_count + token
            inside = self.place > 0
        elif token >= self.own_count:
            ref, row = self.above_ref, token - self.own_count
            inside = self.place < self.places - 1
        elif certain(token, frame):
            return None
        else:
            ref, row = self.own_ref, token
        at = self.place * (RATIO * self.own_count) + frame
        held = (ref[row, 0] <= at) & (at <= ref[row, 1])
        return held if inside is None else held & inside


def head_tiles(tiles, tokens, key_ref, value_ref, head):
    lanes = lanes_at(head, DH)
    for group, first, last in tiles.groups:
        rows = slice((first - tiles.first) * BLOCK, (last - tiles.first) * BLOCK)
        keys, values = key_ref[rows, lanes], value_ref[rows, lanes]
        query_rows = tokens.rows(group, head, False)
        grad_rows = tokens.rows(group, head, True)
        scores = lax.dot_general(keys, query_rows, NT, preferred_element_type=F32)
        slopes = lax.dot_general(values, grad_rows, NT, preferred_element_type=F32)
        yield group, first, last, keys, query_rows, grad_rows, scores, slopes


def piece(array, frame, position):
    return array[frame * BLOCK : (frame + 1) * BLOCK, position * BLOCK : (position + 1) * BLOCK]


def fold(stats, rate):
    tops = [jnp.where(total > 0, top, NEG) for top, total, _ in stats]
    top = functools.reduce(jnp.maximum, tops)
    gains = [jnp.exp2((t - top) * rate) for t in tops]
    total = sum(g * s[1] for g, s in zip(gains, stats))
    weighted = sum(g * s[2] for g, s in zip(gains, stats))
    return top, total, weighted


def tile_stats(bands, tiles_list, tokens, kv_refs, head, rate):
    found = {}
    for tiles, (key_ref, value_ref) in zip(tiles_list, kv_refs):
        for group, first, last, _, _, _, scores, slopes in head_tiles(
            tiles, tokens, key_ref, value_ref, head
        ):
            for position, t in enumerate(group):
                for f in range(first, last):
                    allowed = bands.allowed(t, f)
                    found.setdefault(t, []).append(
                        (allowed, piece(scores, f - first, position), piece(slopes, f - first, position))
                    )
    stats = {}
    for t, entries in found.items():
        shown = [s if a is None else jnp.where(a, s, NEG) for a, s, _ in entries]
        top = jnp.max(functools.reduce(jnp.maximum, shown), axis=0, keepdims=True)
        total = weighted = None
        for (allowed, _, slope), s in zip(entries, shown):
            e = jnp.exp2((s - top) * rate)
            if allowed is not None:
                e = jnp.where(allowed, e, 0.0)
            total = e if total is None else total + e
            weighted = e * slope if weighted is None else weighted + e * slope
        stats[t] = (
            top,
            jnp.sum(total, axis=0, keepdims=True),
            jnp.sum(weighted, axis=0, keepdims=True),
        )
    return stats


def read_stats(ref, head, row):
    return tuple(ref[head, row + i : row + i + 1, :] for i in range(3))


def stat_depth(own_count):
    return -(-3 * (own_count + 2) // 8) * 8


def row_stats(
    band, tiles_list, kvs, queries, grads, below, above, earlier, last, rate
):
    own_count = queries.shape[0] // BLOCK
    columns = queries.shape[1]
    heads = columns // DH
    per = min(PER_STATS, heads)
    depth = stat_depth(own_count)
    count = len(kvs)
    halo = any(t < 0 or t >= own_count for tiles in tiles_list for t in tiles.touched)
    shared = (queries, grads) + ((below, above) if halo else ())
    extra = [] if earlier is None else [earlier]

    def body(*refs):
        bands, refs = Bands(refs[:3], own_count), refs[3:]
        tokens = Tokens(own_count, columns, refs[: len(shared)])
        refs = refs[len(shared) :]
        kv_refs = [refs[2 * i : 2 * i + 2] for i in range(count)]
        rest = refs[2 * count :]
        out_ref = rest[len(extra)]
        even = lax.rem(lax.axis_index(ROWS), 2) == 0

        def step(pair, carry):
            for k in range(per):
                head = pair * per + k
                stats = tile_stats(bands, tiles_list, tokens, kv_refs, head, rate)
                results = []
                for t in range(-1, own_count + 1):
                    mine = [stats[t]] if t in stats else []
                    if extra:
                        mine.append(read_stats(rest[0], head, 3 * (t + 1)))
                    results += mine[0] if len(mine) == 1 else fold(mine, rate)
                blank = [jnp.zeros((1, BLOCK), F32)]
                out_ref[head] = jnp.concatenate(
                    results + blank * (depth - len(results)), axis=0
                )
                if last:
                    lower, upper = results[:6], results[-6:]
                    for ref, flag in zip(rest[len(extra) + 1 :], (even, jnp.logical_not(even))):
                        picked = [jnp.where(flag, u, d) for u, d in zip(upper, lower)]
                        ref[head] = jnp.concatenate(picked + blank * 2, axis=0)
            return carry

        lax.fori_loop(0, heads // per, step, 0)

    frames = sum(kv[0].shape[0] for kv in kvs)
    flat = [array for kv in kvs for array in kv]
    shapes = [jax.ShapeDtypeStruct((heads, depth, BLOCK), F32)]
    if last:
        shapes += [jax.ShapeDtypeStruct((heads, 8, BLOCK), F32)] * 2
    return call(
        body,
        [SCALARS] * 3
        + [HERE] * len(shared)
        + [HERE] * (len(flat) + len(extra)),
        [HERE] * len(shapes),
        shapes,
        [],
        8 * frames * 2 * BLOCK * columns,
        4 * frames * columns + 8 * queries.size,
    )(*band, *shared, *flat, *extra)


def term_block(buffer, at, step, key_ref, value_ref, rows, out_ref):
    term = lax.dot_general(
        key_ref[rows, :], buffer[at, 0, step], NT, preferred_element_type=F32
    ) + lax.dot_general(value_ref[rows, :], buffer[at, 1, step], NT, preferred_element_type=F32)
    out_ref[:, lanes_at(step, buffer.shape[3])] = term.astype(BF16)


def gradients(
    band,
    tiles,
    kv,
    queries,
    grads,
    below,
    above,
    stats,
    swaps,
    key_weight,
    value_weight,
    held,
    deferred,
    totals,
    rate,
    scale,
    group,
):
    own_count = queries.shape[0] // BLOCK
    columns = queries.shape[1]
    heads = columns // DH
    per = min(PER_GRADIENTS, heads)
    frames = kv[0].shape[0]
    touched = tiles.touched
    halo_touched = [t for t in touched if not 0 <= t < own_count]
    shared = (queries, grads) + ((below, above) if halo_touched else ())
    weights = Weights(key_weight, False, group)
    steps, features = weights.steps, weights.features
    loads = held is None
    sources_in = [key_weight, value_weight] if loads else [held]
    defer = not halo_touched
    extra = [] if defer else list(deferred)
    earlier = [] if totals is None else list(totals)
    base = tiles.first * BLOCK
    ahead = min(4, weights.steps)

    def body(*refs):
        bands, refs = Bands(refs[:3], own_count), refs[3:]
        tokens = Tokens(own_count, columns, refs[: len(shared)])
        refs = refs[len(shared) :]
        key_ref, value_ref, stat_ref, even_ref, odd_ref = refs[:5]
        both, refs = refs[5 : 5 + len(sources_in)], refs[5 + len(sources_in) :]
        extra_refs, refs = refs[: len(extra)], refs[len(extra) + len(earlier) :]
        if loads:
            buffer, sems, refs = refs[-2], refs[-1], refs[:-2]
            owners = targets(group)[1:]
            weights.start(both, buffer, sems, owners, ahead)
        else:
            buffer = both[0]
        key_out, value_out, own_out = refs[:3]
        term_outs = refs[3 : 2 + group]
        halo_outs = refs[2 + group :]
        even = lax.rem(lax.axis_index(ROWS), 2) == 0

        def one(head):
            lanes = lanes_at(head, DH)
            rows = {}
            for t in touched:
                parts = [read_stats(stat_ref, head, 3 * (t + 1))]
                if t <= 0:
                    row = 3 * (t + 1)
                    first, second = read_stats(odd_ref, head, row), read_stats(even_ref, head, row)
                    parts.append([jnp.where(even, a, b) for a, b in zip(first, second)])
                if t >= own_count - 1:
                    row = 3 * (t - own_count + 1)
                    first, second = read_stats(even_ref, head, row), read_stats(odd_ref, head, row)
                    parts.append([jnp.where(even, a, b) for a, b in zip(first, second)])
                top, total, weighted = fold(parts, rate)
                rows[t] = (top * rate + jnp.log2(total), weighted / total)
            key_sum = [None] * (tiles.last - tiles.first)
            value_sum = [None] * (tiles.last - tiles.first)
            query_sum = {}
            if extra:
                query_part = lax.dot_general(
                    extra_refs[1][head], extra_refs[0][:, lanes], TN, preferred_element_type=F32
                )
                for t in range(own_count):
                    query_sum[t] = query_part[t * BLOCK : (t + 1) * BLOCK]
            for group_tokens, first, last, keys, query_rows, grad_rows, scores, slopes in head_tiles(
                tiles, tokens, key_ref, value_ref, head
            ):
                low, slope_low = [], []
                for f in range(first, last):
                    low_row, slope_row = [], []
                    for position, t in enumerate(group_tokens):
                        level, delta = rows[t]
                        p = jnp.exp2(piece(scores, f - first, position) * rate - level)
                        d = p * (piece(slopes, f - first, position) - delta) * scale
                        allowed = bands.allowed(t, f)
                        if allowed is not None:
                            p = jnp.where(allowed, p, 0.0)
                            d = jnp.where(allowed, d, 0.0)
                        low_row.append(p.astype(BF16))
                        slope_row.append(d.astype(BF16))
                    low.append(jnp.concatenate(low_row, axis=1))
                    slope_low.append(jnp.concatenate(slope_row, axis=1))
                low = jnp.concatenate(low, axis=0)
                slope_low = jnp.concatenate(slope_low, axis=0)
                key_part = jnp.dot(slope_low, query_rows, preferred_element_type=F32)
                value_part = jnp.dot(low, grad_rows, preferred_element_type=F32)
                if defer:
                    own_out[head] = slope_low
                else:
                    query_part = lax.dot_general(slope_low, keys, TN, preferred_element_type=F32)
                    for position, t in enumerate(group_tokens):
                        part = query_part[position * BLOCK : (position + 1) * BLOCK]
                        query_sum[t] = query_sum[t] + part if t in query_sum else part
                for f in range(first, last):
                    at, cut = f - tiles.first, slice((f - first) * BLOCK, (f - first + 1) * BLOCK)
                    for sums, part in ((key_sum, key_part), (value_sum, value_part)):
                        sums[at] = part[cut] if sums[at] is None else sums[at] + part[cut]
            for at in range(tiles.last - tiles.first):
                cut = slice(base + at * BLOCK, base + (at + 1) * BLOCK)
                key_out[cut, lanes] = key_sum[at].astype(BF16)
                value_out[cut, lanes] = value_sum[at].astype(BF16)
            if not defer:
                for t in range(own_count):
                    own_out[t * BLOCK : (t + 1) * BLOCK, lanes] = query_sum[t]
                for out_ref, t in zip(halo_outs, halo_touched):
                    out_ref[:, lanes] = query_sum[t]

        def step(pair, carry):
            for k in range(per):
                one(pair * per + k)
            if loads:

                @pl.when(pair + ahead < steps)
                def _():
                    weights.wait(both, buffer, sems, owners, pair)
                    weights.start_step(both, buffer, sems, owners, pair + ahead)

            return carry

        lax.fori_loop(0, heads // per, step, 0)
        done = min(heads // per, steps - ahead)
        if loads:
            for j in range(done + ahead, steps):
                weights.start_step(both, buffer, sems, owners, j)

        def term_step(j, carry):
            if loads:

                @pl.when(j >= done)
                def _():
                    weights.wait(both, buffer, sems, owners, j)

            for at, out_ref in enumerate(term_outs):
                term_block(buffer, at, j, key_out, value_out, slice(base, base + frames), out_ref)
            return carry

        lax.fori_loop(0, steps, term_step, 0)

    shapes = (
        [jax.ShapeDtypeStruct((RATIO * own_count * BLOCK, columns), BF16)] * 2
        + [
            jax.ShapeDtypeStruct((heads, frames, own_count * BLOCK), BF16)
            if defer
            else jax.ShapeDtypeStruct((own_count * BLOCK, columns), F32)
        ]
        + [jax.ShapeDtypeStruct((frames, features), BF16)] * (group - 1)
        + [jax.ShapeDtypeStruct((BLOCK, columns), F32)] * len(halo_touched)
        + ([jax.ShapeDtypeStruct(weights.buffer_shape(group - 1), BF16)] if loads else [])
    )
    out = call(
        body,
        [SCALARS] * 3
        + [HERE] * (len(shared) + 5)
        + ([ANYWHERE] * 2 if loads else [HERE])
        + [HERE] * (len(extra) + len(earlier)),
        [HERE] * len(shapes),
        shapes,
        [weights.semaphores(group - 1)] if loads else [],
        20 * frames * 2 * BLOCK * columns + 4 * frames * columns * features * (group - 1),
        8 * frames * columns,
        {8 + len(shared) + len(sources_in) + len(extra) + i: i for i in range(len(earlier))},
    )(*band, *shared, *kv, stats, *swaps, *sources_in, *extra, *earlier)
    halo = dict(zip(halo_touched, out[2 + group :]))
    return out[:2], out[2], out[3 : 2 + group], halo, out[-1] if loads else held


def own_terms(totals, key_weight, value_weight, group):
    rows, columns = totals[0].shape
    weights = Weights(key_weight, False, group)

    def body(key_grad_ref, value_grad_ref, key_ref, value_ref, out_ref, buffer, sems):
        both = key_ref, value_ref
        owners = targets(group)[:1]
        weights.start(both, buffer, sems, owners, WINDOW)

        def step(j, carry):
            weights.advance(both, buffer, sems, owners, j)
            term_block(buffer, 0, j, key_grad_ref, value_grad_ref, slice(0, rows), out_ref)
            return carry

        lax.fori_loop(0, weights.steps, step, 0)

    return call(
        body,
        [HERE] * 2 + [ANYWHERE] * 2,
        HERE,
        jax.ShapeDtypeStruct((rows, weights.features), BF16),
        [weights.scratch(1), weights.semaphores(1)],
        4 * rows * columns * weights.features,
        4 * columns * weights.features,
    )(*totals, key_weight, value_weight)


def finish_queries(low, high, from_below, from_above):
    rows, columns = low.shape
    tall = BLOCK
    steps = rows // tall

    def body(low_ref, high_ref, below_ref, above_ref, out_ref, buffer, sems):
        copies = []
        for i in range(steps):
            cut = slice(i * tall, (i + 1) * tall)
            total = low_ref[cut, :] + high_ref[cut, :]
            if i == 0:
                total = total + below_ref[...]
            if i == steps - 1:
                total = total + above_ref[...]
            buffer[i] = total.astype(BF16)
            copies.append(pltpu.make_async_copy(buffer.at[i], out_ref.at[pl.ds(i * tall, tall), :], sems.at[i]))
            copies[-1].start()
        for copy in copies:
            copy.wait()

    return call(
        body,
        [HERE] * 4,
        ANYWHERE,
        pltpu.HBM((rows, columns), BF16),
        [pltpu.VMEM((steps, tall, columns), BF16), pltpu.SemaphoreType.DMA((steps,))],
        4 * rows * columns,
        12 * rows * columns,
    )(low, high, from_below, from_above)


def add_rows(target, own, arrived, first):
    rows, features = arrived[0].shape
    tall = BLOCK // 2
    steps = rows // tall
    count = len(arrived)

    def body(own_ref, *refs):
        terms = refs[:count]
        out_ref, buffer, sems = refs[-3:]
        copies = []
        for i in range(steps):
            value = own_ref[first + i * tall : first + (i + 1) * tall, :].astype(F32)
            for ref in terms:
                value = value + ref[i * tall : (i + 1) * tall, :].astype(F32)
            buffer[i] = value.astype(BF16)
            copy = pltpu.make_async_copy(
                buffer.at[i], out_ref.at[pl.ds(first + i * tall, tall), :], sems.at[i]
            )
            copy.start()
            copies.append(copy)
        for copy in copies:
            copy.wait()

    extra = [] if target is None else [target]
    return call(
        body,
        [HERE] * (1 + count) + [ANYWHERE] * len(extra),
        ANYWHERE,
        pltpu.HBM(own.shape, own.dtype),
        [pltpu.VMEM((steps, tall, features), BF16), pltpu.SemaphoreType.DMA((steps,))],
        rows * features * count,
        2 * rows * features * (count + 2),
        {1 + count: 0} if extra else None,
    )(own, *arrived, *extra)


def shifted(value, steps):
    count = lax.axis_size(ROWS)
    first, last = (max(0, -steps), min(count, count - steps))
    return lax.ppermute(value, ROWS, [(source, source + steps) for source in range(first, last)])


def swapped(value, first):
    pairs = []
    for at in range(first, lax.axis_size(ROWS) - 1, 2):
        pairs += [(at, at + 1), (at + 1, at)]
    return lax.ppermute(value, ROWS, pairs)


def on_device(encoder_states, key_weight, value_weight, queries, out_grad, band_blocks):
    frames = encoder_states.shape[0]
    tokens = queries.shape[0]
    own_count = tokens // BLOCK
    frame_blocks = frames // BLOCK
    scale = DH ** (-0.5)
    rate = scale * math.log2(math.e)
    group = lax.axis_size("tensor")
    edge = HALO_BLK
    middle = frame_blocks // 2
    cuts = [(0, edge), (frame_blocks - edge, frame_blocks), (edge, middle), (middle, frame_blocks - edge)]
    row_cuts = [(first * BLOCK, last * BLOCK) for first, last in cuts]
    turns = [[(i, (i + k) % group) for i in range(group)] for k in range(1, group)]

    key_weight, value_weight = [
        pltpu.with_memory_space_constraint(w, pltpu.HBM) for w in (key_weight, value_weight)
    ]
    arrived = []
    for rows in take_rows(encoder_states, row_cuts[:1]) + take_rows(encoder_states, row_cuts[1:]):
        arrived.append([lax.ppermute(rows, "tensor", turn) for turn in turns])

    partial, edge_up, edge_down = project_own(
        encoder_states, queries, out_grad, key_weight, value_weight, row_cuts, group
    )
    edge_up, edge_down, band_sent = lax.optimization_barrier((edge_up, edge_down, band_blocks))
    below = shifted(edge_up, 1)
    above = shifted(edge_down, -1)
    band = (shifted(band_sent, 1), band_blocks, shifted(band_sent, -1))

    kvs, held = [], None
    for part, pieces in zip(partial, arrived):
        kv, held = project_rest(part, pieces, key_weight, value_weight, held, group)
        kvs.append(kv)

    tiles = [Tiles(own_count, first, last, i < 2) for i, (first, last) in enumerate(cuts)]
    shared = (queries, out_grad, below, above)
    (stats,) = row_stats(band, tiles[:2], kvs[:2], *shared, None, False, rate)
    (stats,) = row_stats(band, tiles[2:3], kvs[2:3], *shared, stats, False, rate)
    stats, first_swap, second_swap = row_stats(
        band, tiles[3:], kvs[3:], *shared, stats, True, rate
    )
    swaps = (swapped(first_swap, 0), swapped(second_swap, 1))

    out = [None] * 4
    sent = [None] * 4
    totals = away = None
    for i in (2, 3, 0, 1):
        deferred = (kvs[2 + i][0], out[2 + i][1]) if i < 2 else None
        out[i] = gradients(
            band,
            tiles[i],
            kvs[i],
            *shared,
            stats,
            swaps,
            key_weight,
            value_weight,
            away,
            deferred,
            totals,
            rate,
            scale,
            group,
        )
        totals, away = out[i][0], out[i][4]
        sent[i] = [lax.ppermute(term, "tensor", turn) for term, turn in zip(out[i][2], turns)]

    from_below = shifted(out[1][3][own_count], 1)
    from_above = shifted(out[0][3][-1], -1)
    own = own_terms(totals, key_weight, value_weight, group)
    query_grad = finish_queries(out[0][1], out[1][1], from_below, from_above)

    encoder_grad = None
    for i in (2, 3, 0, 1):
        encoder_grad = add_rows(encoder_grad, own, sent[i], row_cuts[i][0])
    return (query_grad, encoder_grad)


def solution(mesh):
    return jax.shard_map(
        on_device,
        mesh=mesh,
        in_specs=(
            P(ROWS, "tensor"),
            P(None, "tensor"),
            P(None, "tensor"),
            P(ROWS, "tensor"),
            P(ROWS, "tensor"),
            P(ROWS, None),
        ),
        out_specs=(P(ROWS, "tensor"), P(ROWS, "tensor")),
        check_vma=False,
    )
```

```python
import functools
import math

import jax
import jax.numpy as jnp
from jax import lax
from jax.experimental import pallas as pl
from jax.experimental.pallas import tpu as pltpu
from jax.sharding import PartitionSpec as P


DH = 128
BLOCK = 128
RATIO = 3
HALO_BLK = 2
NEG = -1e30
WINDOW = 3
PER_STATS = 4
PER_GRADIENTS = 4
ROWS = ("seq", "section")
NT = (((1,), (1,)), ((), ()))
TN = (((0,), (0,)), ((), ()))
F32 = jnp.float32
BF16 = jnp.bfloat16


ANYWHERE = pl.BlockSpec(memory_space=pltpu.HBM)
HERE = pl.BlockSpec(memory_space=pltpu.VMEM)
SCALARS = pl.BlockSpec(memory_space=pltpu.SMEM)


def call(body, in_specs, out_specs, out_shape, scratch, flops, moved, aliases=None):
    return pl.pallas_call(
        body,
        in_specs=in_specs,
        out_specs=out_specs,
        out_shape=out_shape,
        scratch_shapes=scratch,
        input_output_aliases=aliases or {},
        compiler_params=pltpu.CompilerParams(vmem_limit_bytes=limit_of(scratch)),
        cost_estimate=pl.CostEstimate(flops=flops, bytes_accessed=moved, transcendentals=0),
    )


def limit_of(scratch):
    held = 0
    for item in scratch:
        if item.dtype in (BF16, F32):
            held += math.prod(item.shape) * jnp.dtype(item.dtype).itemsize
    return held + 3 * 2**20


def lanes_at(step, wide):
    return pl.ds(pl.multiple_of(step * wide, wide), wide)


class Weights:
    def __init__(self, key_weight, by_columns, group):
        rows, columns = key_weight.shape
        self.features = rows // group
        self.by_columns = by_columns
        if by_columns:
            self.step = min(256, columns)
            self.steps = columns // self.step
            self.block = (self.features, self.step)
        else:
            self.step = min(256, self.features)
            self.steps = self.features // self.step
            self.block = (self.step, columns)

    def buffer_shape(self, count):
        return (count, 2, self.steps) + self.block

    def scratch(self, count):
        return pltpu.VMEM(self.buffer_shape(count), BF16)

    def semaphores(self, count):
        return pltpu.SemaphoreType.DMA((count, 2, self.steps))

    def copy(self, refs, buffer, sems, owner, at, which, step):
        if self.by_columns:
            first = pl.multiple_of(owner * self.features, self.features)
            source = refs[which].at[pl.ds(first, self.features), lanes_at(step, self.step)]
        else:
            first = pl.multiple_of(owner * self.features + step * self.step, self.step)
            source = refs[which].at[pl.ds(first, self.step), :]
        return pltpu.make_async_copy(
            source, buffer.at[at, which, step], sems.at[at, which, step]
        )

    def start_step(self, refs, buffer, sems, owners, step):
        for at, owner in enumerate(owners):
            for which in range(2):
                self.copy(refs, buffer, sems, owner, at, which, step).start()

    def start(self, refs, buffer, sems, owners, window=None):
        for step in range(min(self.steps, window or self.steps)):
            self.start_step(refs, buffer, sems, owners, step)

    def wait(self, refs, buffer, sems, owners, step):
        for at, owner in enumerate(owners):
            for which in range(2):
                self.copy(refs, buffer, sems, owner, at, which, step).wait()

    def advance(self, refs, buffer, sems, owners, step):
        self.wait(refs, buffer, sems, owners, step)

        @pl.when(step + WINDOW < self.steps)
        def _():
            self.start_step(refs, buffer, sems, owners, step + WINDOW)


def sources(group):
    me = lax.axis_index("tensor")
    return [lax.rem(me - k + group, group) for k in range(group)]


def targets(group):
    me = lax.axis_index("tensor")
    return [lax.rem(me + k, group) for k in range(group)]


def take_rows(states, cuts):
    def body(states_ref, *refs):
        outs, sems = refs[:-1], refs[-1]
        copies = []
        for i, (first, last) in enumerate(cuts):
            copies.append(
                pltpu.make_async_copy(states_ref.at[pl.ds(first, last - first), :], outs[i], sems.at[i])
            )
            copies[-1].start()
        for copy in copies:
            copy.wait()

    shapes = [jax.ShapeDtypeStruct((last - first, states.shape[1]), BF16) for first, last in cuts]
    return call(
        body,
        [ANYWHERE],
        [HERE] * len(cuts),
        shapes,
        [pltpu.SemaphoreType.DMA((len(cuts),))],
        0,
        4 * sum(math.prod(shape.shape) for shape in shapes),
    )(pltpu.with_memory_space_constraint(states, pltpu.HBM))


def project_own(states, queries, grads, key_weight, value_weight, cuts, group):
    rows, depth = states.shape
    columns = key_weight.shape[1]
    tokens = queries.shape[0]
    weights = Weights(key_weight, True, group)
    count = len(cuts)

    def body(states_ref, query_ref, grad_ref, key_ref, value_ref, *refs):
        outs = refs[: 2 * count]
        up_ref, down_ref = refs[2 * count : 2 * count + 2]
        buffer, sems = refs[2 * count + 2 :]
        owners = sources(group)[:1]
        both = (key_ref, value_ref)
        weights.start(both, buffer, sems, owners, WINDOW)
        for at, ref in enumerate((query_ref, grad_ref)):
            lanes = slice(at * columns, (at + 1) * columns)
            up_ref[:, lanes] = ref[tokens - BLOCK :, :]
            down_ref[:, lanes] = ref[:BLOCK, :]

        def step(j, carry):
            weights.advance(both, buffer, sems, owners, j)
            for which in range(2):
                product = jnp.dot(
                    states_ref[...], buffer[0, which, j], preferred_element_type=F32
                )
                for piece_at, (first, last) in enumerate(cuts):
                    outs[2 * piece_at + which][:, lanes_at(j, weights.step)] = product[first:last]
            return carry

        lax.fori_loop(0, weights.steps, step, 0)

    shapes = []
    for first, last in cuts:
        shapes += [jax.ShapeDtypeStruct((last - first, columns), F32)] * 2
    edge = jax.ShapeDtypeStruct((BLOCK, 2 * columns), BF16)
    out = call(
        body,
        [HERE] * 3 + [ANYWHERE] * 2,
        [HERE] * (len(shapes) + 2),
        shapes + [edge, edge],
        [weights.scratch(1), weights.semaphores(1)],
        4 * rows * depth * columns,
        2 * rows * depth + 4 * depth * columns,
    )(states, queries, grads, key_weight, value_weight)
    return [(out[2 * i], out[2 * i + 1]) for i in range(count)], out[-2], out[-1]


def project_rest(partial, arrived, key_weight, value_weight, held, group, base=0, height=None, into=None):
    rows, columns = partial[0].shape
    height = height or rows
    earlier = [] if into is None else list(into)
    depth = arrived[0].shape[1]
    count = len(arrived)
    weights = Weights(key_weight, True, group)
    loads = held is None

    def body(key_part, value_part, *refs):
        pieces, refs = refs[:count], refs[count + len(earlier) :]
        if loads:
            both, outs, (buffer, sems) = refs[:2], refs[2:4], refs[4:]
            owners = sources(group)[1:]
            weights.start(both, buffer, sems, owners, WINDOW)
        else:
            buffer, outs = refs[0], refs[1:]

        def step(j, carry):
            if loads:
                weights.advance(both, buffer, sems, owners, j)
            here = lanes_at(j, weights.step)
            for which, part_ref in enumerate((key_part, value_part)):
                total = part_ref[:, here]
                for at in range(count):
                    total = total + jnp.dot(
                        pieces[at][...], buffer[at, which, j], preferred_element_type=F32
                    )
                outs[which][base : base + rows, here] = total.astype(BF16)
            return carry

        lax.fori_loop(0, weights.steps, step, 0)

    shapes = [jax.ShapeDtypeStruct((height, columns), BF16)] * 2
    if loads:
        shapes.append(jax.ShapeDtypeStruct(weights.buffer_shape(count), BF16))
    out = call(
        body,
        [HERE] * (2 + count + len(earlier)) + ([ANYWHERE] * 2 if loads else [HERE]),
        [HERE] * len(shapes),
        shapes,
        [weights.semaphores(count)] if loads else [],
        4 * rows * depth * columns * count,
        4 * depth * columns * count if loads else 2 * rows * columns,
        {2 + count + i: i for i in range(len(earlier))},
    )(*partial, *arrived, *earlier, *((key_weight, value_weight) if loads else (held,)))
    return (out[0], out[1]), (out[2] if loads else held)


def certain(token, frame):
    return RATIO * token - 1 <= frame <= RATIO * token + RATIO


def reaches(token, frame):
    return RATIO * token - HALO_BLK <= frame <= RATIO * token + RATIO - 1 + HALO_BLK


class Tiles:
    def __init__(self, tokens, first, last, halo, origin=None):
        self.first, self.last, self.tokens = first, last, tokens
        self.origin = first if origin is None else origin
        low, high = (-1, tokens + 1) if halo else (0, tokens)
        touched = [
            t for t in range(low, high) if any(reaches(t, f) for f in range(first, last))
        ]
        whole = [t for t in touched if all(reaches(t, f) for f in range(first, last))]
        self.groups = []
        if whole:
            self.groups.append((whole, first, last))
        for t in touched:
            if t not in whole:
                frames = [f for f in range(first, last) if reaches(t, f)]
                self.groups.append(([t], frames[0], frames[-1] + 1))
        self.touched = touched


class Tokens:
    def __init__(self, own_count, columns, refs):
        self.own_count, self.columns = own_count, columns
        self.query_ref, self.grad_ref = refs[:2]
        self.below_ref, self.above_ref = refs[2:] if len(refs) > 2 else (None, None)

    def rows(self, tokens, head, grads):
        own_ref = self.grad_ref if grads else self.query_ref
        lanes = lanes_at(head, DH)
        halo = lanes_at(head + (self.columns // DH if grads else 0), DH)
        pieces = []
        for t in tokens:
            if t < 0:
                pieces.append(self.below_ref[:, halo])
            elif t >= self.own_count:
                pieces.append(self.above_ref[:, halo])
            else:
                pieces.append(own_ref[t * BLOCK : (t + 1) * BLOCK, lanes])
        return pieces[0] if len(pieces) == 1 else jnp.concatenate(pieces, axis=0)


class Bands:
    def __init__(self, refs, own_count):
        self.below_ref, self.own_ref, self.above_ref = refs
        self.own_count = own_count
        self.place, self.places = lax.axis_index(ROWS), lax.axis_size(ROWS)

    def allowed(self, token, frame):
        inside = None
        if token < 0:
            ref, row = self.below_ref, self.own_count + token
            inside = self.place > 0
        elif token >= self.own_count:
            ref, row = self.above_ref, token - self.own_count
            inside = self.place < self.places - 1
        elif certain(token, frame):
            return None
        else:
            ref, row = self.own_ref, token
        at = self.place * (RATIO * self.own_count) + frame
        held = (ref[row, 0] <= at) & (at <= ref[row, 1])
        return held if inside is None else held & inside


def head_tiles(tiles, tokens, key_ref, value_ref, head):
    lanes = lanes_at(head, DH)
    for group, first, last in tiles.groups:
        rows = slice((first - tiles.origin) * BLOCK, (last - tiles.origin) * BLOCK)
        keys, values = key_ref[rows, lanes], value_ref[rows, lanes]
        query_rows = tokens.rows(group, head, False)
        grad_rows = tokens.rows(group, head, True)
        scores = lax.dot_general(keys, query_rows, NT, preferred_element_type=F32)
        slopes = lax.dot_general(values, grad_rows, NT, preferred_element_type=F32)
        yield group, first, last, keys, query_rows, grad_rows, scores, slopes


def piece(array, frame, position):
    return array[frame * BLOCK : (frame + 1) * BLOCK, position * BLOCK : (position + 1) * BLOCK]


def fold(stats, rate):
    tops = [jnp.where(total > 0, top, NEG) for top, total, _ in stats]
    top = functools.reduce(jnp.maximum, tops)
    gains = [jnp.exp2((t - top) * rate) for t in tops]
    total = sum(g * s[1] for g, s in zip(gains, stats))
    weighted = sum(g * s[2] for g, s in zip(gains, stats))
    return top, total, weighted


def tile_stats(bands, tiles_list, tokens, kv_refs, head, rate, kept):
    found = {}
    for tiles, (key_ref, value_ref) in zip(tiles_list, kv_refs):
        for group, first, last, _, _, _, scores, slopes in head_tiles(
            tiles, tokens, key_ref, value_ref, head
        ):
            if kept:
                kept[0][head] = scores
                kept[1][head] = slopes
            for position, t in enumerate(group):
                for f in range(first, last):
                    allowed = bands.allowed(t, f)
                    found.setdefault(t, []).append(
                        (allowed, piece(scores, f - first, position), piece(slopes, f - first, position))
                    )
    stats = {}
    for t, entries in found.items():
        shown = [s if a is None else jnp.where(a, s, NEG) for a, s, _ in entries]
        top = jnp.max(functools.reduce(jnp.maximum, shown), axis=0, keepdims=True)
        total = weighted = None
        for (allowed, _, slope), s in zip(entries, shown):
            e = jnp.exp2((s - top) * rate)
            if allowed is not None:
                e = jnp.where(allowed, e, 0.0)
            total = e if total is None else total + e
            weighted = e * slope if weighted is None else weighted + e * slope
        stats[t] = (
            top,
            jnp.sum(total, axis=0, keepdims=True),
            jnp.sum(weighted, axis=0, keepdims=True),
        )
    return stats


def read_stats(ref, head, row):
    return tuple(ref[head, row + i : row + i + 1, :] for i in range(3))


def stat_depth(own_count):
    return -(-3 * (own_count + 2) // 8) * 8


def row_stats(
    band, tiles_list, kvs, queries, grads, below, above, earlier, last, keep, rate
):
    own_count = queries.shape[0] // BLOCK
    columns = queries.shape[1]
    heads = columns // DH
    per = min(PER_STATS, heads)
    depth = stat_depth(own_count)
    count = len(kvs)
    halo = any(t < 0 or t >= own_count for tiles in tiles_list for t in tiles.touched)
    shared = (queries, grads) + ((below, above) if halo else ())
    extra = [] if earlier is None else [earlier]

    def body(*refs):
        bands, refs = Bands(refs[:3], own_count), refs[3:]
        tokens = Tokens(own_count, columns, refs[: len(shared)])
        refs = refs[len(shared) :]
        kv_refs = [refs[2 * i : 2 * i + 2] for i in range(count)]
        rest = refs[2 * count :]
        out_ref = rest[len(extra)]
        kept = rest[-2:] if keep else ()
        even = lax.rem(lax.axis_index(ROWS), 2) == 0

        def step(pair, carry):
            for k in range(per):
                head = pair * per + k
                stats = tile_stats(bands, tiles_list, tokens, kv_refs, head, rate, kept)
                results = []
                for t in range(-1, own_count + 1):
                    mine = [stats[t]] if t in stats else []
                    if extra:
                        mine.append(read_stats(rest[0], head, 3 * (t + 1)))
                    results += mine[0] if len(mine) == 1 else fold(mine, rate)
                blank = [jnp.zeros((1, BLOCK), F32)]
                out_ref[head] = jnp.concatenate(
                    results + blank * (depth - len(results)), axis=0
                )
                if last:
                    lower, upper = results[:6], results[-6:]
                    for ref, flag in zip(rest[len(extra) + 1 : len(extra) + 3], (even, jnp.logical_not(even))):
                        picked = [jnp.where(flag, u, d) for u, d in zip(upper, lower)]
                        ref[head] = jnp.concatenate(picked + blank * 2, axis=0)
            return carry

        lax.fori_loop(0, heads // per, step, 0)

    frames = sum(kv[0].shape[0] for kv in kvs)
    flat = [array for kv in kvs for array in kv]
    shapes = [jax.ShapeDtypeStruct((heads, depth, BLOCK), F32)]
    if last:
        shapes += [jax.ShapeDtypeStruct((heads, 8, BLOCK), F32)] * 2
    if keep:
        ((group, first, end),) = tiles_list[0].groups
        shapes += [jax.ShapeDtypeStruct((heads, (end - first) * BLOCK, len(group) * BLOCK), F32)] * 2
    return call(
        body,
        [SCALARS] * 3
        + [HERE] * len(shared)
        + [HERE] * (len(flat) + len(extra)),
        [HERE] * len(shapes),
        shapes,
        [],
        8 * frames * 2 * BLOCK * columns,
        4 * frames * columns + 8 * queries.size,
    )(*band, *shared, *flat, *extra)


def term_block(buffer, at, step, key_ref, value_ref, rows, out_ref):
    term = lax.dot_general(
        key_ref[rows, :], buffer[at, 0, step], NT, preferred_element_type=F32
    ) + lax.dot_general(value_ref[rows, :], buffer[at, 1, step], NT, preferred_element_type=F32)
    out_ref[:, lanes_at(step, buffer.shape[3])] = term.astype(BF16)


def gradients(
    band,
    tiles,
    kv,
    queries,
    grads,
    below,
    above,
    stats,
    swaps,
    key_weight,
    value_weight,
    held,
    deferred,
    kept,
    totals,
    rate,
    scale,
    group,
):
    own_count = queries.shape[0] // BLOCK
    columns = queries.shape[1]
    heads = columns // DH
    per = min(PER_GRADIENTS, heads)
    frames = kv[0].shape[0]
    touched = tiles.touched
    halo_touched = [t for t in touched if not 0 <= t < own_count]
    shared = (queries, grads) + ((below, above) if halo_touched else ())
    weights = Weights(key_weight, False, group)
    steps, features = weights.steps, weights.features
    loads = held is None
    sources_in = [key_weight, value_weight] if loads else [held]
    defer = not halo_touched
    extra = [] if defer else list(deferred)
    known = [array for _, *arrays in kept for array in arrays]
    earlier = [] if totals is None else list(totals)
    base = tiles.first * BLOCK
    ahead = min(4, weights.steps)

    def body(*refs):
        bands, refs = Bands(refs[:3], own_count), refs[3:]
        tokens = Tokens(own_count, columns, refs[: len(shared)])
        refs = refs[len(shared) :]
        key_ref, value_ref, stat_ref, even_ref, odd_ref = refs[:5]
        both, refs = refs[5 : 5 + len(sources_in)], refs[5 + len(sources_in) :]
        extra_refs, refs = refs[: len(extra)], refs[len(extra) :]
        known_refs, refs = refs[: len(known)], refs[len(known) + len(earlier) :]
        if loads:
            buffer, sems, refs = refs[-2], refs[-1], refs[:-2]
            owners = targets(group)[1:]
            weights.start(both, buffer, sems, owners, ahead)
        else:
            buffer = both[0]
        key_out, value_out, own_out = refs[:3]
        term_outs = refs[3 : 2 + group]
        halo_outs = refs[2 + group :]
        even = lax.rem(lax.axis_index(ROWS), 2) == 0

        def one(head):
            lanes = lanes_at(head, DH)
            rows = {}
            for t in touched:
                parts = [read_stats(stat_ref, head, 3 * (t + 1))]
                if t <= 0:
                    row = 3 * (t + 1)
                    first, second = read_stats(odd_ref, head, row), read_stats(even_ref, head, row)
                    parts.append([jnp.where(even, a, b) for a, b in zip(first, second)])
                if t >= own_count - 1:
                    row = 3 * (t - own_count + 1)
                    first, second = read_stats(even_ref, head, row), read_stats(odd_ref, head, row)
                    parts.append([jnp.where(even, a, b) for a, b in zip(first, second)])
                top, total, weighted = fold(parts, rate)
                rows[t] = (top * rate + jnp.log2(total), weighted / total)
            key_sum = [None] * (tiles.last - tiles.first)
            value_sum = [None] * (tiles.last - tiles.first)
            query_sum = {}
            if extra:
                query_part = lax.dot_general(
                    extra_refs[1][head], extra_refs[0][:, lanes], TN, preferred_element_type=F32
                )
                for t in range(own_count):
                    query_sum[t] = query_part[t * BLOCK : (t + 1) * BLOCK]
            for group_tokens, first, last in tiles.groups:
                cut = slice((first - tiles.origin) * BLOCK, (last - tiles.origin) * BLOCK)
                query_rows = tokens.rows(group_tokens, head, False)
                grad_rows = tokens.rows(group_tokens, head, True)
                if known:
                    scores = [known_refs[2 * i][head] for i in range(len(kept))]
                    slopes = [known_refs[2 * i + 1][head] for i in range(len(kept))]
                    scores, slopes = jnp.concatenate(scores), jnp.concatenate(slopes)
                else:
                    keys, values = key_ref[cut, lanes], value_ref[cut, lanes]
                    scores = lax.dot_general(keys, query_rows, NT, preferred_element_type=F32)
                    slopes = lax.dot_general(values, grad_rows, NT, preferred_element_type=F32)
                low, slope_low = [], []
                for f in range(first, last):
                    low_row, slope_row = [], []
                    for position, t in enumerate(group_tokens):
                        level, delta = rows[t]
                        p = jnp.exp2(piece(scores, f - first, position) * rate - level)
                        d = p * (piece(slopes, f - first, position) - delta) * scale
                        allowed = bands.allowed(t, f)
                        if allowed is not None:
                            p = jnp.where(allowed, p, 0.0)
                            d = jnp.where(allowed, d, 0.0)
                        low_row.append(p.astype(BF16))
                        slope_row.append(d.astype(BF16))
                    low.append(jnp.concatenate(low_row, axis=1))
                    slope_low.append(jnp.concatenate(slope_row, axis=1))
                low = jnp.concatenate(low, axis=0)
                slope_low = jnp.concatenate(slope_low, axis=0)
                key_part = jnp.dot(slope_low, query_rows, preferred_element_type=F32)
                value_part = jnp.dot(low, grad_rows, preferred_element_type=F32)
                if defer:
                    own_out[head] = slope_low
                else:
                    query_part = lax.dot_general(slope_low, keys, TN, preferred_element_type=F32)
                    for position, t in enumerate(group_tokens):
                        part = query_part[position * BLOCK : (position + 1) * BLOCK]
                        query_sum[t] = query_sum[t] + part if t in query_sum else part
                for f in range(first, last):
                    at, cut = f - tiles.first, slice((f - first) * BLOCK, (f - first + 1) * BLOCK)
                    for sums, part in ((key_sum, key_part), (value_sum, value_part)):
                        sums[at] = part[cut] if sums[at] is None else sums[at] + part[cut]
            for at in range(tiles.last - tiles.first):
                cut = slice(base + at * BLOCK, base + (at + 1) * BLOCK)
                key_out[cut, lanes] = key_sum[at].astype(BF16)
                value_out[cut, lanes] = value_sum[at].astype(BF16)
            if not defer:
                for t in range(own_count):
                    part = query_sum[t] if t in query_sum else jnp.zeros((BLOCK, DH), F32)
                    own_out[t * BLOCK : (t + 1) * BLOCK, lanes] = part
                for out_ref, t in zip(halo_outs, halo_touched):
                    out_ref[:, lanes] = query_sum[t]

        def step(pair, carry):
            for k in range(per):
                one(pair * per + k)
            if loads:

                @pl.when(pair + ahead < steps)
                def _():
                    weights.wait(both, buffer, sems, owners, pair)
                    weights.start_step(both, buffer, sems, owners, pair + ahead)

            return carry

        lax.fori_loop(0, heads // per, step, 0)
        done = min(heads // per, steps - ahead)
        if loads:
            for j in range(done + ahead, steps):
                weights.start_step(both, buffer, sems, owners, j)

        def term_step(j, carry):
            if loads:

                @pl.when(j >= done)
                def _():
                    weights.wait(both, buffer, sems, owners, j)

            for at, out_ref in enumerate(term_outs):
                term_block(buffer, at, j, key_out, value_out, slice(base, base + frames), out_ref)
            return carry

        lax.fori_loop(0, steps, term_step, 0)

    shapes = (
        [jax.ShapeDtypeStruct((RATIO * own_count * BLOCK, columns), BF16)] * 2
        + [
            jax.ShapeDtypeStruct((heads, frames, own_count * BLOCK), BF16)
            if defer
            else jax.ShapeDtypeStruct((own_count * BLOCK, columns), F32)
        ]
        + [jax.ShapeDtypeStruct((frames, features), BF16)] * (group - 1)
        + [jax.ShapeDtypeStruct((BLOCK, columns), F32)] * len(halo_touched)
        + ([jax.ShapeDtypeStruct(weights.buffer_shape(group - 1), BF16)] if loads else [])
    )
    out = call(
        body,
        [SCALARS] * 3
        + [HERE] * (len(shared) + 5)
        + ([ANYWHERE] * 2 if loads else [HERE])
        + [HERE] * (len(extra) + len(known) + len(earlier)),
        [HERE] * len(shapes),
        shapes,
        [weights.semaphores(group - 1)] if loads else [],
        20 * frames * 2 * BLOCK * columns + 4 * frames * columns * features * (group - 1),
        8 * frames * columns,
        {
            8 + len(shared) + len(sources_in) + len(extra) + len(known) + i: i
            for i in range(len(earlier))
        },
    )(*band, *shared, *kv, stats, *swaps, *sources_in, *extra, *known, *earlier)
    halo = dict(zip(halo_touched, out[2 + group :]))
    return out[:2], out[2], out[3 : 2 + group], halo, out[-1] if loads else held


def own_terms(totals, key_weight, value_weight, group):
    rows, columns = totals[0].shape
    weights = Weights(key_weight, False, group)

    def body(key_grad_ref, value_grad_ref, key_ref, value_ref, out_ref, buffer, sems):
        both = key_ref, value_ref
        owners = targets(group)[:1]
        weights.start(both, buffer, sems, owners, WINDOW)

        def step(j, carry):
            weights.advance(both, buffer, sems, owners, j)
            term_block(buffer, 0, j, key_grad_ref, value_grad_ref, slice(0, rows), out_ref)
            return carry

        lax.fori_loop(0, weights.steps, step, 0)

    return call(
        body,
        [HERE] * 2 + [ANYWHERE] * 2,
        HERE,
        jax.ShapeDtypeStruct((rows, weights.features), BF16),
        [weights.scratch(1), weights.semaphores(1)],
        4 * rows * columns * weights.features,
        4 * columns * weights.features,
    )(*totals, key_weight, value_weight)


def finish_queries(low, high, from_below, from_above):
    rows, columns = low.shape
    tall = BLOCK
    steps = rows // tall

    def body(low_ref, high_ref, below_ref, above_ref, out_ref, buffer, sems):
        copies = []
        for i in range(steps):
            cut = slice(i * tall, (i + 1) * tall)
            total = low_ref[cut, :] + high_ref[cut, :]
            if i == 0:
                total = total + below_ref[...]
            if i == steps - 1:
                total = total + above_ref[...]
            buffer[i] = total.astype(BF16)
            copies.append(pltpu.make_async_copy(buffer.at[i], out_ref.at[pl.ds(i * tall, tall), :], sems.at[i]))
            copies[-1].start()
        for copy in copies:
            copy.wait()

    return call(
        body,
        [HERE] * 4,
        ANYWHERE,
        pltpu.HBM((rows, columns), BF16),
        [pltpu.VMEM((steps, tall, columns), BF16), pltpu.SemaphoreType.DMA((steps,))],
        4 * rows * columns,
        12 * rows * columns,
    )(low, high, from_below, from_above)


def add_rows(target, own, arrived, first):
    rows, features = arrived[0].shape
    tall = BLOCK // 2
    steps = rows // tall
    count = len(arrived)

    def body(own_ref, *refs):
        terms = refs[:count]
        out_ref, buffer, sems = refs[-3:]
        copies = []
        for i in range(steps):
            value = own_ref[first + i * tall : first + (i + 1) * tall, :].astype(F32)
            for ref in terms:
                value = value + ref[i * tall : (i + 1) * tall, :].astype(F32)
            buffer[i] = value.astype(BF16)
            copy = pltpu.make_async_copy(
                buffer.at[i], out_ref.at[pl.ds(first + i * tall, tall), :], sems.at[i]
            )
            copy.start()
            copies.append(copy)
        for copy in copies:
            copy.wait()

    extra = [] if target is None else [target]
    return call(
        body,
        [HERE] * (1 + count) + [ANYWHERE] * len(extra),
        ANYWHERE,
        pltpu.HBM(own.shape, own.dtype),
        [pltpu.VMEM((steps, tall, features), BF16), pltpu.SemaphoreType.DMA((steps,))],
        rows * features * count,
        2 * rows * features * (count + 2),
        {1 + count: 0} if extra else None,
    )(own, *arrived, *extra)


def shifted(value, steps):
    count = lax.axis_size(ROWS)
    first, last = (max(0, -steps), min(count, count - steps))
    return lax.ppermute(value, ROWS, [(source, source + steps) for source in range(first, last)])


def swapped(value, first):
    pairs = []
    for at in range(first, lax.axis_size(ROWS) - 1, 2):
        pairs += [(at, at + 1), (at + 1, at)]
    return lax.ppermute(value, ROWS, pairs)


def on_device(encoder_states, key_weight, value_weight, queries, out_grad, band_blocks):
    frames = encoder_states.shape[0]
    tokens = queries.shape[0]
    own_count = tokens // BLOCK
    frame_blocks = frames // BLOCK
    scale = DH ** (-0.5)
    rate = scale * math.log2(math.e)
    group = lax.axis_size("tensor")
    edge = HALO_BLK
    middle = frame_blocks // 2
    cuts = [(0, edge), (frame_blocks - edge, frame_blocks), (edge, middle), (middle, frame_blocks - edge)]
    row_cuts = [(first * BLOCK, last * BLOCK) for first, last in cuts]
    turns = [[(i, (i + k) % group) for i in range(group)] for k in range(1, group)]

    key_weight, value_weight = [
        pltpu.with_memory_space_constraint(w, pltpu.HBM) for w in (key_weight, value_weight)
    ]
    arrived = []
    for rows in take_rows(encoder_states, row_cuts[:1]) + take_rows(encoder_states, row_cuts[1:]):
        arrived.append([lax.ppermute(rows, "tensor", turn) for turn in turns])

    partial, edge_up, edge_down = project_own(
        encoder_states, queries, out_grad, key_weight, value_weight, row_cuts, group
    )
    edge_up, edge_down, band_sent = lax.optimization_barrier((edge_up, edge_down, band_blocks))
    below = shifted(edge_up, 1)
    above = shifted(edge_down, -1)
    band = (shifted(band_sent, 1), band_blocks, shifted(band_sent, -1))

    def rest(i, held, **place):
        return project_rest(partial[i], arrived[i], key_weight, value_weight, held, group, **place)

    def statistics(*where, **what):
        return row_stats(band, *where, queries, out_grad, below, above, *what.values(), rate)

    low_kv, held = rest(0, None)
    high_kv, held = rest(1, held)
    low_tiles, high_tiles = [Tiles(own_count, first, last, True) for first, last in cuts[:2]]
    inner = [Tiles(own_count, first, last, False, edge) for first, last in cuts[2:]]
    inner_tiles = Tiles(own_count, edge, frame_blocks - edge, False)
    (stats,) = statistics([low_tiles, high_tiles], [low_kv, high_kv], earlier=None, last=False, keep=False)
    height = (frame_blocks - 2 * edge) * BLOCK
    kv, held = rest(2, held, height=height)
    stats, *first_kept = statistics(inner[:1], [kv], earlier=stats, last=False, keep=True)
    kv, stats = lax.optimization_barrier((kv, stats))
    inner_kv, held = rest(3, held, base=(middle - edge) * BLOCK, height=height, into=kv)
    stats, first_swap, second_swap, *second_kept = statistics(
        inner[1:], [inner_kv], earlier=stats, last=True, keep=True
    )
    kept = [(edge, *first_kept), (middle, *second_kept)]
    swaps = (swapped(first_swap, 0), swapped(second_swap, 1))

    chunks = [(inner_tiles, inner_kv), (low_tiles, low_kv), (high_tiles, high_kv)]
    shared = (queries, out_grad, below, above, stats, swaps, key_weight, value_weight)
    out, sent = [], []
    totals = away = deferred = None
    for i, (tiles, kv) in enumerate(chunks):
        out.append(
            gradients(
                band,
                tiles,
                kv,
                *shared,
                away,
                deferred,
                () if i else kept,
                totals,
                rate,
                scale,
                group,
            )
        )
        totals, away = out[i][0], out[i][4]
        deferred = () if i else (inner_kv[0], out[0][1])
        sent.append([lax.ppermute(term, "tensor", turn) for term, turn in zip(out[i][2], turns)])

    from_below = shifted(out[2][3][own_count], 1)
    from_above = shifted(out[1][3][-1], -1)
    own = own_terms(totals, key_weight, value_weight, group)
    query_grad = finish_queries(out[1][1], out[2][1], from_below, from_above)

    encoder_grad = None
    for i, (tiles, _) in enumerate(chunks):
        encoder_grad = add_rows(encoder_grad, own, sent[i], tiles.first * BLOCK)
    return (query_grad, encoder_grad)


def solution(mesh):
    return jax.shard_map(
        on_device,
        mesh=mesh,
        in_specs=(
            P(ROWS, "tensor"),
            P(None, "tensor"),
            P(None, "tensor"),
            P(ROWS, "tensor"),
            P(ROWS, "tensor"),
            P(ROWS, None),
        ),
        out_specs=(P(ROWS, "tensor"), P(ROWS, "tensor")),
        check_vma=False,
    )
```

```python
import functools
import math

import jax
import jax.numpy as jnp
from jax import lax
from jax.experimental import pallas as pl
from jax.experimental.pallas import tpu as pltpu
from jax.sharding import PartitionSpec as P


DH = 128
BLOCK = 128
RATIO = 3
HALO_BLK = 2
NEG = -1e30
WINDOW = 3
PER_STATS = 8
PER_GRADIENTS = 8
ROWS = ("seq", "section")
NT = (((1,), (1,)), ((), ()))
TN = (((0,), (0,)), ((), ()))
F32 = jnp.float32
BF16 = jnp.bfloat16


ANYWHERE = pl.BlockSpec(memory_space=pltpu.HBM)
HERE = pl.BlockSpec(memory_space=pltpu.VMEM)
SCALARS = pl.BlockSpec(memory_space=pltpu.SMEM)


def call(body, in_specs, out_specs, out_shape, scratch, flops, moved, aliases=None):
    return pl.pallas_call(
        body,
        in_specs=in_specs,
        out_specs=out_specs,
        out_shape=out_shape,
        scratch_shapes=scratch,
        input_output_aliases=aliases or {},
        compiler_params=pltpu.CompilerParams(vmem_limit_bytes=limit_of(scratch)),
        cost_estimate=pl.CostEstimate(flops=flops, bytes_accessed=moved, transcendentals=0),
    )


def limit_of(scratch):
    held = 0
    for item in scratch:
        if item.dtype in (BF16, F32):
            held += math.prod(item.shape) * jnp.dtype(item.dtype).itemsize
    return held + 3 * 2**20


def lanes_at(step, wide):
    return pl.ds(pl.multiple_of(step * wide, wide), wide)


class Weights:
    def __init__(self, key_weight, by_columns, group):
        rows, columns = key_weight.shape
        self.features = rows // group
        self.by_columns = by_columns
        if by_columns:
            self.step = min(256, columns)
            self.steps = columns // self.step
            self.block = (self.features, self.step)
        else:
            self.step = min(256, self.features)
            self.steps = self.features // self.step
            self.block = (self.step, columns)

    def buffer_shape(self, count):
        return (count, 2, self.steps) + self.block

    def scratch(self, count):
        return pltpu.VMEM(self.buffer_shape(count), BF16)

    def semaphores(self, count):
        return pltpu.SemaphoreType.DMA((count, 2, self.steps))

    def copy(self, refs, buffer, sems, owner, at, which, step):
        if self.by_columns:
            first = pl.multiple_of(owner * self.features, self.features)
            source = refs[which].at[pl.ds(first, self.features), lanes_at(step, self.step)]
        else:
            first = pl.multiple_of(owner * self.features + step * self.step, self.step)
            source = refs[which].at[pl.ds(first, self.step), :]
        return pltpu.make_async_copy(
            source, buffer.at[at, which, step], sems.at[at, which, step]
        )

    def start_step(self, refs, buffer, sems, owners, step):
        for at, owner in enumerate(owners):
            for which in range(2):
                self.copy(refs, buffer, sems, owner, at, which, step).start()

    def start(self, refs, buffer, sems, owners, window=None):
        for step in range(min(self.steps, window or self.steps)):
            self.start_step(refs, buffer, sems, owners, step)

    def wait(self, refs, buffer, sems, owners, step):
        for at, owner in enumerate(owners):
            for which in range(2):
                self.copy(refs, buffer, sems, owner, at, which, step).wait()

    def advance(self, refs, buffer, sems, owners, step):
        self.wait(refs, buffer, sems, owners, step)

        @pl.when(step + WINDOW < self.steps)
        def _():
            self.start_step(refs, buffer, sems, owners, step + WINDOW)


def sources(group):
    me = lax.axis_index("tensor")
    return [lax.rem(me - k + group, group) for k in range(group)]


def targets(group):
    me = lax.axis_index("tensor")
    return [lax.rem(me + k, group) for k in range(group)]


def take_rows(states, cuts):
    def body(states_ref, *refs):
        outs, sems = refs[:-1], refs[-1]
        copies = []
        for i, (first, last) in enumerate(cuts):
            copies.append(
                pltpu.make_async_copy(states_ref.at[pl.ds(first, last - first), :], outs[i], sems.at[i])
            )
            copies[-1].start()
        for copy in copies:
            copy.wait()

    shapes = [jax.ShapeDtypeStruct((last - first, states.shape[1]), BF16) for first, last in cuts]
    return call(
        body,
        [ANYWHERE],
        [HERE] * len(cuts),
        shapes,
        [pltpu.SemaphoreType.DMA((len(cuts),))],
        0,
        4 * sum(math.prod(shape.shape) for shape in shapes),
    )(pltpu.with_memory_space_constraint(states, pltpu.HBM))


def take_edges(queries, grads):
    tokens, columns = queries.shape

    def body(query_ref, grad_ref, up_ref, down_ref, sems):
        copies = []
        for i, (first, out_ref) in enumerate(((tokens - BLOCK, up_ref), (0, down_ref))):
            for at, ref in enumerate((query_ref, grad_ref)):
                copies.append(
                    pltpu.make_async_copy(
                        ref.at[pl.ds(first, BLOCK), :],
                        out_ref.at[:, pl.ds(at * columns, columns)],
                        sems.at[2 * i + at],
                    )
                )
                copies[-1].start()
        for copy in copies:
            copy.wait()

    edge = jax.ShapeDtypeStruct((BLOCK, 2 * columns), BF16)
    return call(
        body, [ANYWHERE] * 2, [HERE] * 2, [edge, edge], [pltpu.SemaphoreType.DMA((4,))], 0, 16 * BLOCK * columns
    )(*[pltpu.with_memory_space_constraint(a, pltpu.HBM) for a in (queries, grads)])


def project_own(states, key_weight, value_weight, cuts, group):
    rows, depth = states.shape
    columns = key_weight.shape[1]
    weights = Weights(key_weight, True, group)
    count = len(cuts)

    def body(states_ref, key_ref, value_ref, *refs):
        outs = refs[: 2 * count]
        buffer, sems = refs[2 * count :]
        owners = sources(group)[:1]
        both = (key_ref, value_ref)
        weights.start(both, buffer, sems, owners, WINDOW)

        def step(j, carry):
            weights.advance(both, buffer, sems, owners, j)
            for which in range(2):
                product = jnp.dot(
                    states_ref[...], buffer[0, which, j], preferred_element_type=F32
                )
                for piece_at, (first, last) in enumerate(cuts):
                    outs[2 * piece_at + which][:, lanes_at(j, weights.step)] = product[first:last]
            return carry

        lax.fori_loop(0, weights.steps, step, 0)

    shapes = []
    for first, last in cuts:
        shapes += [jax.ShapeDtypeStruct((last - first, columns), F32)] * 2
    out = call(
        body,
        [HERE] + [ANYWHERE] * 2,
        [HERE] * len(shapes),
        shapes,
        [weights.scratch(1), weights.semaphores(1)],
        4 * rows * depth * columns,
        2 * rows * depth + 4 * depth * columns,
    )(states, key_weight, value_weight)
    return [(out[2 * i], out[2 * i + 1]) for i in range(count)]


def project_rest(partial, arrived, key_weight, value_weight, held, group, base=0, height=None, into=None):
    rows, columns = partial[0].shape
    height = height or rows
    earlier = [] if into is None else list(into)
    depth = arrived[0].shape[1]
    count = len(arrived)
    weights = Weights(key_weight, True, group)
    loads = held is None

    def body(key_part, value_part, *refs):
        pieces, refs = refs[:count], refs[count + len(earlier) :]
        if loads:
            both, outs, (buffer, sems) = refs[:2], refs[2:4], refs[4:]
            owners = sources(group)[1:]
            weights.start(both, buffer, sems, owners, WINDOW)
        else:
            buffer, outs = refs[0], refs[1:]

        def step(j, carry):
            if loads:
                weights.advance(both, buffer, sems, owners, j)
            here = lanes_at(j, weights.step)
            for which, part_ref in enumerate((key_part, value_part)):
                total = part_ref[:, here]
                for at in range(count):
                    total = total + jnp.dot(
                        pieces[at][...], buffer[at, which, j], preferred_element_type=F32
                    )
                outs[which][base : base + rows, here] = total.astype(BF16)
            return carry

        lax.fori_loop(0, weights.steps, step, 0)

    shapes = [jax.ShapeDtypeStruct((height, columns), BF16)] * 2
    if loads:
        shapes.append(jax.ShapeDtypeStruct(weights.buffer_shape(count), BF16))
    out = call(
        body,
        [HERE] * (2 + count + len(earlier)) + ([ANYWHERE] * 2 if loads else [HERE]),
        [HERE] * len(shapes),
        shapes,
        [weights.semaphores(count)] if loads else [],
        4 * rows * depth * columns * count,
        4 * depth * columns * count if loads else 2 * rows * columns,
        {2 + count + i: i for i in range(len(earlier))},
    )(*partial, *arrived, *earlier, *((key_weight, value_weight) if loads else (held,)))
    return (out[0], out[1]), (out[2] if loads else held)


def certain(token, frame):
    return RATIO * token - 1 <= frame <= RATIO * token + RATIO


def reaches(token, frame):
    return RATIO * token - HALO_BLK <= frame <= RATIO * token + RATIO - 1 + HALO_BLK


class Tiles:
    def __init__(self, tokens, first, last, halo, origin=None):
        self.first, self.last, self.tokens = first, last, tokens
        self.origin = first if origin is None else origin
        low, high = (-1, tokens + 1) if halo else (0, tokens)
        touched = [
            t for t in range(low, high) if any(reaches(t, f) for f in range(first, last))
        ]
        whole = [t for t in touched if all(reaches(t, f) for f in range(first, last))]
        self.groups = []
        if whole:
            self.groups.append((whole, first, last))
        for t in touched:
            if t not in whole:
                frames = [f for f in range(first, last) if reaches(t, f)]
                self.groups.append(([t], frames[0], frames[-1] + 1))
        self.touched = touched


class Tokens:
    def __init__(self, own_count, columns, refs):
        self.own_count, self.columns = own_count, columns
        self.query_ref, self.grad_ref = refs[:2]
        self.below_ref, self.above_ref = refs[2:] if len(refs) > 2 else (None, None)

    def rows(self, tokens, head, grads):
        own_ref = self.grad_ref if grads else self.query_ref
        lanes = lanes_at(head, DH)
        halo = lanes_at(head + (self.columns // DH if grads else 0), DH)
        pieces = []
        for t in tokens:
            if t < 0:
                pieces.append(self.below_ref[:, halo])
            elif t >= self.own_count:
                pieces.append(self.above_ref[:, halo])
            else:
                pieces.append(own_ref[t * BLOCK : (t + 1) * BLOCK, lanes])
        return pieces[0] if len(pieces) == 1 else jnp.concatenate(pieces, axis=0)


class Bands:
    def __init__(self, refs, own_count):
        self.below_ref, self.own_ref, self.above_ref = refs
        self.own_count = own_count
        self.place, self.places = lax.axis_index(ROWS), lax.axis_size(ROWS)

    def allowed(self, token, frame):
        inside = None
        if token < 0:
            ref, row = self.below_ref, self.own_count + token
            inside = self.place > 0
        elif token >= self.own_count:
            ref, row = self.above_ref, token - self.own_count
            inside = self.place < self.places - 1
        elif certain(token, frame):
            return None
        else:
            ref, row = self.own_ref, token
        at = self.place * (RATIO * self.own_count) + frame
        held = (ref[row, 0] <= at) & (at <= ref[row, 1])
        return held if inside is None else held & inside


def head_tiles(tiles, tokens, key_ref, value_ref, head):
    lanes = lanes_at(head, DH)
    for group, first, last in tiles.groups:
        rows = slice((first - tiles.origin) * BLOCK, (last - tiles.origin) * BLOCK)
        keys, values = key_ref[rows, lanes], value_ref[rows, lanes]
        query_rows = tokens.rows(group, head, False)
        grad_rows = tokens.rows(group, head, True)
        scores = lax.dot_general(keys, query_rows, NT, preferred_element_type=F32)
        slopes = lax.dot_general(values, grad_rows, NT, preferred_element_type=F32)
        yield group, first, last, keys, query_rows, grad_rows, scores, slopes


def piece(array, frame, position):
    return array[frame * BLOCK : (frame + 1) * BLOCK, position * BLOCK : (position + 1) * BLOCK]


def fold(stats, rate):
    tops = [jnp.where(total > 0, top, NEG) for top, total, _ in stats]
    top = functools.reduce(jnp.maximum, tops)
    gains = [jnp.exp2((t - top) * rate) for t in tops]
    total = sum(g * s[1] for g, s in zip(gains, stats))
    weighted = sum(g * s[2] for g, s in zip(gains, stats))
    return top, total, weighted


def tile_stats(bands, tiles_list, tokens, kv_refs, head, rate, kept):
    found = {}
    for tiles, (key_ref, value_ref) in zip(tiles_list, kv_refs):
        for group, first, last, _, _, _, scores, slopes in head_tiles(
            tiles, tokens, key_ref, value_ref, head
        ):
            if kept:
                kept[0][head] = scores
                kept[1][head] = slopes
            for position, t in enumerate(group):
                for f in range(first, last):
                    allowed = bands.allowed(t, f)
                    found.setdefault(t, []).append(
                        (allowed, piece(scores, f - first, position), piece(slopes, f - first, position))
                    )
    stats = {}
    for t, entries in found.items():
        shown = [s if a is None else jnp.where(a, s, NEG) for a, s, _ in entries]
        top = jnp.max(functools.reduce(jnp.maximum, shown), axis=0, keepdims=True)
        total = weighted = None
        for (allowed, _, slope), s in zip(entries, shown):
            e = jnp.exp2((s - top) * rate)
            if allowed is not None:
                e = jnp.where(allowed, e, 0.0)
            total = e if total is None else total + e
            weighted = e * slope if weighted is None else weighted + e * slope
        stats[t] = (
            top,
            jnp.sum(total, axis=0, keepdims=True),
            jnp.sum(weighted, axis=0, keepdims=True),
        )
    return stats


def read_stats(ref, head, row):
    return tuple(ref[head, row + i : row + i + 1, :] for i in range(3))


def stat_depth(own_count):
    return -(-3 * (own_count + 2) // 8) * 8


def row_stats(
    band, tiles_list, kvs, queries, grads, below, above, earlier, send, keep, rate
):
    own_count = queries.shape[0] // BLOCK
    columns = queries.shape[1]
    heads = columns // DH
    per = min(PER_STATS, heads)
    depth = stat_depth(own_count)
    count = len(kvs)
    halo = any(t < 0 or t >= own_count for tiles in tiles_list for t in tiles.touched)
    shared = (queries, grads) + ((below, above) if halo else ())
    extra = [] if earlier is None else [earlier]

    def body(*refs):
        bands, refs = Bands(refs[:3], own_count), refs[3:]
        tokens = Tokens(own_count, columns, refs[: len(shared)])
        refs = refs[len(shared) :]
        kv_refs = [refs[2 * i : 2 * i + 2] for i in range(count)]
        rest = refs[2 * count :]
        out_ref = rest[len(extra)]
        kept = rest[-2:] if keep else ()
        even = lax.rem(lax.axis_index(ROWS), 2) == 0

        def step(pair, carry):
            for k in range(per):
                head = pair * per + k
                stats = tile_stats(bands, tiles_list, tokens, kv_refs, head, rate, kept)
                results = []
                blank = jnp.zeros((1, BLOCK), F32)
                for t in range(-1, own_count + 1):
                    mine = [stats[t]] if t in stats else []
                    if extra:
                        mine.append(read_stats(rest[0], head, 3 * (t + 1)))
                    if not mine:
                        mine = [(blank, blank, blank)]
                    results += mine[0] if len(mine) == 1 else fold(mine, rate)
                out_ref[head] = jnp.concatenate(
                    results + [blank] * (depth - len(results)), axis=0
                )
                if send:
                    upper, lower = [results[3 * (t + 1) : 3 * (t + 2)] for t in send]
                    for ref, flag in zip(rest[len(extra) + 1 : len(extra) + 3], (even, jnp.logical_not(even))):
                        picked = [jnp.where(flag, u, d) for u, d in zip(upper, lower)]
                        ref[head] = jnp.concatenate(picked + [blank] * 5, axis=0)
            return carry

        lax.fori_loop(0, heads // per, step, 0)

    frames = sum(kv[0].shape[0] for kv in kvs)
    flat = [array for kv in kvs for array in kv]
    shapes = [jax.ShapeDtypeStruct((heads, depth, BLOCK), F32)]
    if send:
        shapes += [jax.ShapeDtypeStruct((heads, 8, BLOCK), F32)] * 2
    if keep:
        ((group, first, end),) = tiles_list[0].groups
        shapes += [jax.ShapeDtypeStruct((heads, (end - first) * BLOCK, len(group) * BLOCK), F32)] * 2
    return call(
        body,
        [SCALARS] * 3
        + [HERE] * len(shared)
        + [HERE] * (len(flat) + len(extra)),
        [HERE] * len(shapes),
        shapes,
        [],
        8 * frames * 2 * BLOCK * columns,
        4 * frames * columns + 8 * queries.size,
    )(*band, *shared, *flat, *extra)


def term_block(buffer, at, step, key_ref, value_ref, rows, out_ref):
    term = lax.dot_general(
        key_ref[rows, :], buffer[at, 0, step], NT, preferred_element_type=F32
    ) + lax.dot_general(value_ref[rows, :], buffer[at, 1, step], NT, preferred_element_type=F32)
    out_ref[:, lanes_at(step, buffer.shape[3])] = term.astype(BF16)


def gradients(
    band,
    tiles,
    kv,
    queries,
    grads,
    below,
    above,
    stats,
    swaps,
    key_weight,
    value_weight,
    held,
    deferred,
    kept,
    totals,
    rate,
    scale,
    group,
):
    own_count = queries.shape[0] // BLOCK
    columns = queries.shape[1]
    heads = columns // DH
    per = min(PER_GRADIENTS, heads)
    frames = kv[0].shape[0]
    touched = tiles.touched
    halo_touched = [t for t in touched if not 0 <= t < own_count]
    shared = (queries, grads) + ((below, above) if halo_touched else ())
    weights = Weights(key_weight, False, group)
    steps, features = weights.steps, weights.features
    loads = held is None
    sources_in = [key_weight, value_weight] if loads else [held]
    defer = not halo_touched
    extra = [] if defer else list(deferred)
    known = [array for _, *arrays in kept for array in arrays]
    earlier = [] if totals is None else list(totals)
    base = tiles.first * BLOCK
    ahead = min(4, weights.steps)

    def body(*refs):
        bands, refs = Bands(refs[:3], own_count), refs[3:]
        tokens = Tokens(own_count, columns, refs[: len(shared)])
        refs = refs[len(shared) :]
        key_ref, value_ref, stat_ref = refs[:3]
        swap_refs, refs = refs[3 : 3 + len(swaps)], refs[3 + len(swaps) :]
        both, refs = refs[: len(sources_in)], refs[len(sources_in) :]
        extra_refs, refs = refs[: len(extra)], refs[len(extra) :]
        known_refs, refs = refs[: len(known)], refs[len(known) + len(earlier) :]
        if loads:
            buffer, sems, refs = refs[-2], refs[-1], refs[:-2]
            owners = targets(group)[1:]
            weights.start(both, buffer, sems, owners, ahead)
        else:
            buffer = both[0]
        key_out, value_out, own_out = refs[:3]
        term_outs = refs[3 : 2 + group]
        halo_outs = refs[2 + group :]
        even = lax.rem(lax.axis_index(ROWS), 2) == 0

        def one(head):
            lanes = lanes_at(head, DH)
            rows = {}
            for t in touched:
                parts = [read_stats(stat_ref, head, 3 * (t + 1))]
                even_ref, odd_ref = swap_refs[:2] if 0 <= t < own_count else swap_refs[2:]
                first, second = read_stats(even_ref, head, 0), read_stats(odd_ref, head, 0)
                if t <= 0:
                    parts.append([jnp.where(even, b, a) for a, b in zip(first, second)])
                if t >= own_count - 1:
                    parts.append([jnp.where(even, a, b) for a, b in zip(first, second)])
                top, total, weighted = fold(parts, rate)
                rows[t] = (top * rate + jnp.log2(total), weighted / total)
            key_sum = [None] * (tiles.last - tiles.first)
            value_sum = [None] * (tiles.last - tiles.first)
            query_sum = {}
            if extra:
                query_part = lax.dot_general(
                    extra_refs[1][head], extra_refs[0][:, lanes], TN, preferred_element_type=F32
                )
                for t in range(own_count):
                    query_sum[t] = query_part[t * BLOCK : (t + 1) * BLOCK]
            for group_tokens, first, last in tiles.groups:
                cut = slice((first - tiles.origin) * BLOCK, (last - tiles.origin) * BLOCK)
                query_rows = tokens.rows(group_tokens, head, False)
                grad_rows = tokens.rows(group_tokens, head, True)
                if known:
                    scores = [known_refs[2 * i][head] for i in range(len(kept))]
                    slopes = [known_refs[2 * i + 1][head] for i in range(len(kept))]
                    scores, slopes = jnp.concatenate(scores), jnp.concatenate(slopes)
                else:
                    keys, values = key_ref[cut, lanes], value_ref[cut, lanes]
                    scores = lax.dot_general(keys, query_rows, NT, preferred_element_type=F32)
                    slopes = lax.dot_general(values, grad_rows, NT, preferred_element_type=F32)
                low, slope_low = [], []
                for f in range(first, last):
                    low_row, slope_row = [], []
                    for position, t in enumerate(group_tokens):
                        level, delta = rows[t]
                        p = jnp.exp2(piece(scores, f - first, position) * rate - level)
                        d = p * (piece(slopes, f - first, position) - delta) * scale
                        allowed = bands.allowed(t, f)
                        if allowed is not None:
                            p = jnp.where(allowed, p, 0.0)
                            d = jnp.where(allowed, d, 0.0)
                        low_row.append(p.astype(BF16))
                        slope_row.append(d.astype(BF16))
                    low.append(jnp.concatenate(low_row, axis=1))
                    slope_low.append(jnp.concatenate(slope_row, axis=1))
                low = jnp.concatenate(low, axis=0)
                slope_low = jnp.concatenate(slope_low, axis=0)
                key_part = jnp.dot(slope_low, query_rows, preferred_element_type=F32)
                value_part = jnp.dot(low, grad_rows, preferred_element_type=F32)
                if defer:
                    own_out[head] = slope_low
                else:
                    query_part = lax.dot_general(slope_low, keys, TN, preferred_element_type=F32)
                    for position, t in enumerate(group_tokens):
                        part = query_part[position * BLOCK : (position + 1) * BLOCK]
                        query_sum[t] = query_sum[t] + part if t in query_sum else part
                for f in range(first, last):
                    at, cut = f - tiles.first, slice((f - first) * BLOCK, (f - first + 1) * BLOCK)
                    for sums, part in ((key_sum, key_part), (value_sum, value_part)):
                        sums[at] = part[cut] if sums[at] is None else sums[at] + part[cut]
            for at in range(tiles.last - tiles.first):
                cut = slice(base + at * BLOCK, base + (at + 1) * BLOCK)
                key_out[cut, lanes] = key_sum[at].astype(BF16)
                value_out[cut, lanes] = value_sum[at].astype(BF16)
            if not defer:
                for t in range(own_count):
                    part = query_sum[t] if t in query_sum else jnp.zeros((BLOCK, DH), F32)
                    own_out[t * BLOCK : (t + 1) * BLOCK, lanes] = part
                for out_ref, t in zip(halo_outs, halo_touched):
                    out_ref[:, lanes] = query_sum[t]

        def step(pair, carry):
            for k in range(per):
                one(pair * per + k)
            if loads:

                @pl.when(pair + ahead < steps)
                def _():
                    weights.wait(both, buffer, sems, owners, pair)
                    weights.start_step(both, buffer, sems, owners, pair + ahead)

            return carry

        lax.fori_loop(0, heads // per, step, 0)
        done = min(heads // per, steps - ahead)
        if loads:
            for j in range(done + ahead, steps):
                weights.start_step(both, buffer, sems, owners, j)

        def term_step(j, carry):
            if loads:

                @pl.when(j >= done)
                def _():
                    weights.wait(both, buffer, sems, owners, j)

            for at, out_ref in enumerate(term_outs):
                term_block(buffer, at, j, key_out, value_out, slice(base, base + frames), out_ref)
            return carry

        lax.fori_loop(0, steps, term_step, 0)

    shapes = (
        [jax.ShapeDtypeStruct((RATIO * own_count * BLOCK, columns), BF16)] * 2
        + [
            jax.ShapeDtypeStruct((heads, frames, own_count * BLOCK), BF16)
            if defer
            else jax.ShapeDtypeStruct((own_count * BLOCK, columns), F32)
        ]
        + [jax.ShapeDtypeStruct((frames, features), BF16)] * (group - 1)
        + [jax.ShapeDtypeStruct((BLOCK, columns), F32)] * len(halo_touched)
        + ([jax.ShapeDtypeStruct(weights.buffer_shape(group - 1), BF16)] if loads else [])
    )
    out = call(
        body,
        [SCALARS] * 3
        + [HERE] * (len(shared) + 3 + len(swaps))
        + ([ANYWHERE] * 2 if loads else [HERE])
        + [HERE] * (len(extra) + len(known) + len(earlier)),
        [HERE] * len(shapes),
        shapes,
        [weights.semaphores(group - 1)] if loads else [],
        20 * frames * 2 * BLOCK * columns + 4 * frames * columns * features * (group - 1),
        8 * frames * columns,
        {
            6 + len(swaps) + len(shared) + len(sources_in) + len(extra) + len(known) + i: i
            for i in range(len(earlier))
        },
    )(*band, *shared, *kv, stats, *swaps, *sources_in, *extra, *known, *earlier)
    halo = dict(zip(halo_touched, out[2 + group :]))
    return out[:2], out[2], out[3 : 2 + group], halo, out[-1] if loads else held


def own_terms(totals, key_weight, value_weight, group):
    rows, columns = totals[0].shape
    weights = Weights(key_weight, False, group)

    def body(key_grad_ref, value_grad_ref, key_ref, value_ref, out_ref, buffer, sems):
        both = key_ref, value_ref
        owners = targets(group)[:1]
        weights.start(both, buffer, sems, owners, WINDOW)

        def step(j, carry):
            weights.advance(both, buffer, sems, owners, j)
            term_block(buffer, 0, j, key_grad_ref, value_grad_ref, slice(0, rows), out_ref)
            return carry

        lax.fori_loop(0, weights.steps, step, 0)

    return call(
        body,
        [HERE] * 2 + [ANYWHERE] * 2,
        HERE,
        jax.ShapeDtypeStruct((rows, weights.features), BF16),
        [weights.scratch(1), weights.semaphores(1)],
        4 * rows * columns * weights.features,
        4 * columns * weights.features,
    )(*totals, key_weight, value_weight)


def finish_queries(low, high, from_below, from_above):
    rows, columns = low.shape
    tall = BLOCK
    steps = rows // tall

    def body(low_ref, high_ref, below_ref, above_ref, out_ref, buffer, sems):
        copies = []
        for i in range(steps):
            cut = slice(i * tall, (i + 1) * tall)
            total = low_ref[cut, :] + high_ref[cut, :]
            if i == 0:
                total = total + below_ref[...]
            if i == steps - 1:
                total = total + above_ref[...]
            buffer[i] = total.astype(BF16)
            copies.append(pltpu.make_async_copy(buffer.at[i], out_ref.at[pl.ds(i * tall, tall), :], sems.at[i]))
            copies[-1].start()
        for copy in copies:
            copy.wait()

    return call(
        body,
        [HERE] * 4,
        ANYWHERE,
        pltpu.HBM((rows, columns), BF16),
        [pltpu.VMEM((steps, tall, columns), BF16), pltpu.SemaphoreType.DMA((steps,))],
        4 * rows * columns,
        12 * rows * columns,
    )(low, high, from_below, from_above)


def add_rows(target, own, arrived, first):
    rows, features = arrived[0].shape
    tall = BLOCK // 2
    steps = rows // tall
    count = len(arrived)

    def body(own_ref, *refs):
        terms = refs[:count]
        out_ref, buffer, sems = refs[-3:]
        copies = []
        for i in range(steps):
            value = own_ref[first + i * tall : first + (i + 1) * tall, :].astype(F32)
            for ref in terms:
                value = value + ref[i * tall : (i + 1) * tall, :].astype(F32)
            buffer[i] = value.astype(BF16)
            copy = pltpu.make_async_copy(
                buffer.at[i], out_ref.at[pl.ds(first + i * tall, tall), :], sems.at[i]
            )
            copy.start()
            copies.append(copy)
        for copy in copies:
            copy.wait()

    extra = [] if target is None else [target]
    return call(
        body,
        [HERE] * (1 + count) + [ANYWHERE] * len(extra),
        ANYWHERE,
        pltpu.HBM(own.shape, own.dtype),
        [pltpu.VMEM((steps, tall, features), BF16), pltpu.SemaphoreType.DMA((steps,))],
        rows * features * count,
        2 * rows * features * (count + 2),
        {1 + count: 0} if extra else None,
    )(own, *arrived, *extra)


def shifted(value, steps):
    count = lax.axis_size(ROWS)
    first, last = (max(0, -steps), min(count, count - steps))
    return lax.ppermute(value, ROWS, [(source, source + steps) for source in range(first, last)])


def swapped(value, first):
    pairs = []
    for at in range(first, lax.axis_size(ROWS) - 1, 2):
        pairs += [(at, at + 1), (at + 1, at)]
    return lax.ppermute(value, ROWS, pairs)


def on_device(encoder_states, key_weight, value_weight, queries, out_grad, band_blocks):
    frames = encoder_states.shape[0]
    tokens = queries.shape[0]
    own_count = tokens // BLOCK
    frame_blocks = frames // BLOCK
    scale = DH ** (-0.5)
    rate = scale * math.log2(math.e)
    group = lax.axis_size("tensor")
    edge = HALO_BLK
    middle = frame_blocks // 2
    cuts = [(0, edge), (frame_blocks - edge, frame_blocks), (edge, middle), (middle, frame_blocks - edge)]
    row_cuts = [(first * BLOCK, last * BLOCK) for first, last in cuts]
    turns = [[(i, (i + k) % group) for i in range(group)] for k in range(1, group)]

    key_weight, value_weight = [
        pltpu.with_memory_space_constraint(w, pltpu.HBM) for w in (key_weight, value_weight)
    ]
    arrived = []
    for rows in take_rows(encoder_states, row_cuts[:1]) + take_rows(encoder_states, row_cuts[1:]):
        arrived.append([lax.ppermute(rows, "tensor", turn) for turn in turns])

    edge_up, edge_down = take_edges(queries, out_grad)
    below = shifted(edge_up, 1)
    above = shifted(edge_down, -1)
    band = (shifted(band_blocks, 1), band_blocks, shifted(band_blocks, -1))

    partial = project_own(encoder_states, key_weight, value_weight, row_cuts, group)

    def rest(i, held, **place):
        return project_rest(partial[i], arrived[i], key_weight, value_weight, held, group, **place)

    def statistics(*where, **what):
        return row_stats(band, *where, queries, out_grad, below, above, *what.values(), rate)

    def exchange(arrays):
        return tuple(swapped(array, first) for first, array in enumerate(arrays))

    low_tiles, high_tiles = [Tiles(own_count, first, last, True) for first, last in cuts[:2]]
    inner = [Tiles(own_count, first, last, False, edge) for first, last in cuts[2:]]
    inner_tiles = Tiles(own_count, edge, frame_blocks - edge, False)
    low_kv, held = rest(0, None)
    (stats,) = statistics([low_tiles], [low_kv], earlier=None, send=None, keep=False)
    high_kv, held = rest(1, held)
    stats, *outer = statistics([high_tiles], [high_kv], earlier=stats, send=(own_count, -1), keep=False)
    early = exchange(outer)
    height = (frame_blocks - 2 * edge) * BLOCK
    kv, held = rest(2, held, height=height)
    stats, *first_kept = statistics(inner[:1], [kv], earlier=stats, send=None, keep=True)
    kv, stats = lax.optimization_barrier((kv, stats))
    inner_kv, held = rest(3, held, base=(middle - edge) * BLOCK, height=height, into=kv)
    stats, first_own, second_own, *second_kept = statistics(
        inner[1:], [inner_kv], earlier=stats, send=(own_count - 1, 0), keep=True
    )
    late = exchange((first_own, second_own))
    kept = [(edge, *first_kept), (middle, *second_kept)]

    chunks = [(inner_tiles, inner_kv), (low_tiles, low_kv), (high_tiles, high_kv)]
    shared = (queries, out_grad, below, above, stats)
    out, sent = [], []
    totals = away = deferred = None
    for i, (tiles, kv) in enumerate(chunks):
        out.append(
            gradients(
                band,
                tiles,
                kv,
                *shared,
                early + late if i else early,
                key_weight,
                value_weight,
                away,
                deferred,
                () if i else kept,
                totals,
                rate,
                scale,
                group,
            )
        )
        totals, away = out[i][0], out[i][4]
        deferred = (inner_kv[0], out[0][1]) if i == 1 else ()
        sent.append([lax.ppermute(term, "tensor", turn) for term, turn in zip(out[i][2], turns)])

    from_below = shifted(out[2][3][own_count], 1)
    from_above = shifted(out[1][3][-1], -1)
    own = own_terms(totals, key_weight, value_weight, group)
    query_grad = finish_queries(out[1][1], out[2][1], from_below, from_above)

    encoder_grad = None
    for i, (tiles, _) in enumerate(chunks):
        encoder_grad = add_rows(encoder_grad, own, sent[i], tiles.first * BLOCK)
    return (query_grad, encoder_grad)


def solution(mesh):
    return jax.shard_map(
        on_device,
        mesh=mesh,
        in_specs=(
            P(ROWS, "tensor"),
            P(None, "tensor"),
            P(None, "tensor"),
            P(ROWS, "tensor"),
            P(ROWS, "tensor"),
            P(ROWS, None),
        ),
        out_specs=(P(ROWS, "tensor"), P(ROWS, "tensor")),
        check_vma=False,
    )
```

```python
import functools
import math

import jax
import jax.numpy as jnp
from jax import lax
from jax.experimental import pallas as pl
from jax.experimental.pallas import tpu as pltpu
from jax.sharding import PartitionSpec as P


DH = 128
BLOCK = 128
RATIO = 3
HALO_BLK = 2
NEG = -1e30
WINDOW = 3
PER_STATS = 8
PER_LAST = 16
PER_GRADIENTS = 8
UNROLL = 4
ROWS = ("seq", "section")
NT = (((1,), (1,)), ((), ()))
TN = (((0,), (0,)), ((), ()))
F32 = jnp.float32
BF16 = jnp.bfloat16


ANYWHERE = pl.BlockSpec(memory_space=pltpu.HBM)
HERE = pl.BlockSpec(memory_space=pltpu.VMEM)
SCALARS = pl.BlockSpec(memory_space=pltpu.SMEM)


def call(body, in_specs, out_specs, out_shape, scratch, flops, moved, aliases=None):
    return pl.pallas_call(
        body,
        in_specs=in_specs,
        out_specs=out_specs,
        out_shape=out_shape,
        scratch_shapes=scratch,
        input_output_aliases=aliases or {},
        compiler_params=pltpu.CompilerParams(vmem_limit_bytes=limit_of(scratch)),
        cost_estimate=pl.CostEstimate(flops=flops, bytes_accessed=moved, transcendentals=0),
    )


def limit_of(scratch):
    held = 0
    for item in scratch:
        if item.dtype in (BF16, F32):
            held += math.prod(item.shape) * jnp.dtype(item.dtype).itemsize
    return held + 3 * 2**20


def lanes_at(step, wide):
    return pl.ds(pl.multiple_of(step * wide, wide), wide)


class Weights:
    def __init__(self, key_weight, by_columns, group, span=None):
        rows, columns = key_weight.shape
        self.features = rows // group
        self.by_columns = by_columns
        if by_columns:
            self.step = min(256, columns)
            self.steps = columns // self.step
            self.block = (self.features, self.step)
        else:
            self.step = min(256, max(self.features // 4, BLOCK))
            self.steps = self.features // self.step
            self.block = (self.step, columns)
        self.first, last = span or (0, self.steps)
        self.steps = last - self.first

    def buffer_shape(self, count):
        return (count, 2, self.steps) + self.block

    def scratch(self, count):
        return pltpu.VMEM(self.buffer_shape(count), BF16)

    def semaphores(self, count):
        return pltpu.SemaphoreType.DMA((count, 2, self.steps))

    def copy(self, refs, buffer, sems, owner, at, which, step):
        if self.by_columns:
            first = pl.multiple_of(owner * self.features, self.features)
            source = refs[which].at[
                pl.ds(first, self.features), lanes_at(step + self.first, self.step)
            ]
        else:
            first = pl.multiple_of(owner * self.features + (step + self.first) * self.step, self.step)
            source = refs[which].at[pl.ds(first, self.step), :]
        return pltpu.make_async_copy(
            source, buffer.at[at, which, step], sems.at[at, which, step]
        )

    def start_step(self, refs, buffer, sems, owners, step):
        for at, owner in enumerate(owners):
            for which in range(2):
                self.copy(refs, buffer, sems, owner, at, which, step).start()

    def start(self, refs, buffer, sems, owners, window=None):
        for step in range(min(self.steps, window or self.steps)):
            self.start_step(refs, buffer, sems, owners, step)

    def wait(self, refs, buffer, sems, owners, step):
        for at, owner in enumerate(owners):
            for which in range(2):
                self.copy(refs, buffer, sems, owner, at, which, step).wait()

    def advance(self, refs, buffer, sems, owners, step):
        self.wait(refs, buffer, sems, owners, step)

        @pl.when(step + WINDOW < self.steps)
        def _():
            self.start_step(refs, buffer, sems, owners, step + WINDOW)


def sources(group):
    me = lax.axis_index("tensor")
    return [lax.rem(me - k + group, group) for k in range(group)]


def targets(group):
    me = lax.axis_index("tensor")
    return [lax.rem(me + k, group) for k in range(group)]


def take_parts(states, cuts):
    def body(states_ref, *refs):
        outs, sems = refs[:-1], refs[-1]
        copies = []
        for i, (first, last, left, right) in enumerate(cuts):
            part = states_ref.at[pl.ds(first, last - first), pl.ds(left, right - left)]
            copies.append(pltpu.make_async_copy(part, outs[i], sems.at[i]))
            copies[-1].start()
        for copy in copies:
            copy.wait()

    shapes = [
        jax.ShapeDtypeStruct((last - first, right - left), BF16) for first, last, left, right in cuts
    ]
    return call(
        body,
        [ANYWHERE],
        [HERE] * len(cuts),
        shapes,
        [pltpu.SemaphoreType.DMA((len(cuts),))],
        0,
        4 * sum(math.prod(shape.shape) for shape in shapes),
    )(pltpu.with_memory_space_constraint(states, pltpu.HBM))


def take_edges(queries, grads):
    tokens, columns = queries.shape

    def body(query_ref, grad_ref, up_ref, down_ref, sems):
        copies = []
        for i, (first, out_ref) in enumerate(((tokens - BLOCK, up_ref), (0, down_ref))):
            for at, ref in enumerate((query_ref, grad_ref)):
                copies.append(
                    pltpu.make_async_copy(
                        ref.at[pl.ds(first, BLOCK), :],
                        out_ref.at[:, pl.ds(at * columns, columns)],
                        sems.at[2 * i + at],
                    )
                )
                copies[-1].start()
        for copy in copies:
            copy.wait()

    edge = jax.ShapeDtypeStruct((BLOCK, 2 * columns), BF16)
    return call(
        body, [ANYWHERE] * 2, [HERE] * 2, [edge, edge], [pltpu.SemaphoreType.DMA((4,))], 0, 16 * BLOCK * columns
    )(*[pltpu.with_memory_space_constraint(a, pltpu.HBM) for a in (queries, grads)])


def project_own(states, key_weight, value_weight, cuts, group):
    rows, depth = states.shape
    columns = key_weight.shape[1]
    weights = Weights(key_weight, True, group)
    count = len(cuts)

    def body(states_ref, key_ref, value_ref, *refs):
        outs = refs[: 2 * count]
        buffer, sems = refs[2 * count :]
        owners = sources(group)[:1]
        both = (key_ref, value_ref)
        weights.start(both, buffer, sems, owners, WINDOW)

        def step(j, carry):
            weights.advance(both, buffer, sems, owners, j)
            for which in range(2):
                product = jnp.dot(
                    states_ref[...], buffer[0, which, j], preferred_element_type=F32
                )
                for piece_at, (first, last) in enumerate(cuts):
                    outs[2 * piece_at + which][:, lanes_at(j, weights.step)] = product[first:last]
            return carry

        lax.fori_loop(0, weights.steps, step, 0)

    shapes = []
    for first, last in cuts:
        shapes += [jax.ShapeDtypeStruct((last - first, columns), F32)] * 2
    out = call(
        body,
        [HERE] + [ANYWHERE] * 2,
        [HERE] * len(shapes),
        shapes,
        [weights.scratch(1), weights.semaphores(1)],
        4 * rows * depth * columns,
        2 * rows * depth + 4 * depth * columns,
    )(states, key_weight, value_weight)
    return [(out[2 * i], out[2 * i + 1]) for i in range(count)]


def project_rest(
    partial, arrived, key_weight, value_weight, held, group, left=0, final=True, away=None, base=0, height=None, into=None
):
    rows, columns = partial[0].shape
    height = height or rows
    earlier = [] if into is None else list(into)
    depth = arrived[0].shape[1]
    count = len(arrived)
    weights = Weights(key_weight, True, group)
    later = Weights(key_weight, False, group, away) if away else None
    loads = held is None
    used = [key_weight, value_weight] if loads or away else []

    def body(key_part, value_part, *refs):
        pieces, refs = refs[:count], refs[count + len(earlier) :]
        both, refs = refs[: len(used)], refs[len(used) :]
        owners = sources(group)[1:]
        others = targets(group)[1:]
        if loads:
            outs, (buffer, sems) = refs[:2], refs[2:]
            weights.start(both, buffer, sems, owners, WINDOW)
        else:
            buffer, outs, rest = refs[0], refs[1:3], refs[3:]
        if away:
            later.start(both, *rest, others)

        def step(j, carry):
            if loads:
                weights.advance(both, buffer, sems, owners, j)
            here = lanes_at(j, weights.step)
            for which, part_ref in enumerate((key_part, value_part)):
                total = part_ref[:, here]
                for at in range(count):
                    total = total + jnp.dot(
                        pieces[at][...],
                        buffer[at, which, j, left : left + depth, :],
                        preferred_element_type=F32,
                    )
                outs[which][base : base + rows, here] = total.astype(outs[which].dtype)
            return carry

        lax.fori_loop(0, weights.steps, step, 0, unroll=1 if loads or rows > BLOCK else UNROLL)
        if away:
            for j in range(later.steps):
                later.wait(both, *rest, others, j)

    shapes = [jax.ShapeDtypeStruct((height, columns), BF16 if final else F32)] * 2
    if loads:
        shapes.append(jax.ShapeDtypeStruct(weights.buffer_shape(count), BF16))
    if away:
        shapes.append(jax.ShapeDtypeStruct(later.buffer_shape(count), BF16))
    semaphores = [weights.semaphores(count)] if loads else [later.semaphores(count)] if away else []
    aliases = {2 + count + i: i for i in range(len(earlier))} if final else {0: 0, 1: 1}
    out = call(
        body,
        [HERE] * (2 + count + len(earlier)) + [ANYWHERE] * len(used) + [HERE] * (0 if loads else 1),
        [HERE] * len(shapes),
        shapes,
        semaphores,
        4 * rows * depth * columns * count,
        4 * depth * columns * count if loads else 2 * rows * columns,
        aliases,
    )(*partial, *arrived, *earlier, *used, *(() if loads else (held,)))
    return (out[0], out[1]), out[2] if loads or away else None


def away_spans(key_weight, group):
    total = Weights(key_weight, False, group).steps
    first = total // 4
    second = first + (total - first) // 2
    return [(0, first), (first, second), (second, total)]


def certain(token, frame):
    return RATIO * token - 1 <= frame <= RATIO * token + RATIO


def reaches(token, frame):
    return RATIO * token - HALO_BLK <= frame <= RATIO * token + RATIO - 1 + HALO_BLK


class Tiles:
    def __init__(self, tokens, first, last, halo, origin=None):
        self.first, self.last, self.tokens = first, last, tokens
        self.origin = first if origin is None else origin
        low, high = (-1, tokens + 1) if halo else (0, tokens)
        touched = [
            t for t in range(low, high) if any(reaches(t, f) for f in range(first, last))
        ]
        whole = [t for t in touched if all(reaches(t, f) for f in range(first, last))]
        self.groups = []
        if whole:
            self.groups.append((whole, first, last))
        for t in touched:
            if t not in whole:
                frames = [f for f in range(first, last) if reaches(t, f)]
                self.groups.append(([t], frames[0], frames[-1] + 1))
        self.touched = touched


class Tokens:
    def __init__(self, own_count, columns, refs):
        self.own_count, self.columns = own_count, columns
        self.query_ref, self.grad_ref = refs[:2]
        self.below_ref, self.above_ref = refs[2:] if len(refs) > 2 else (None, None)

    def rows(self, tokens, head, grads):
        own_ref = self.grad_ref if grads else self.query_ref
        lanes = lanes_at(head, DH)
        halo = lanes_at(head + (self.columns // DH if grads else 0), DH)
        pieces = []
        for t in tokens:
            if t < 0:
                pieces.append(self.below_ref[:, halo])
            elif t >= self.own_count:
                pieces.append(self.above_ref[:, halo])
            else:
                pieces.append(own_ref[t * BLOCK : (t + 1) * BLOCK, lanes])
        return pieces[0] if len(pieces) == 1 else jnp.concatenate(pieces, axis=0)


class Bands:
    def __init__(self, refs, own_count):
        self.below_ref, self.own_ref, self.above_ref = refs
        self.own_count = own_count
        self.place, self.places = lax.axis_index(ROWS), lax.axis_size(ROWS)

    def allowed(self, token, frame):
        inside = None
        if token < 0:
            ref, row = self.below_ref, self.own_count + token
            inside = self.place > 0
        elif token >= self.own_count:
            ref, row = self.above_ref, token - self.own_count
            inside = self.place < self.places - 1
        elif certain(token, frame):
            return None
        else:
            ref, row = self.own_ref, token
        at = self.place * (RATIO * self.own_count) + frame
        held = (ref[row, 0] <= at) & (at <= ref[row, 1])
        return held if inside is None else held & inside


def head_tiles(tiles, tokens, key_ref, value_ref, head):
    lanes = lanes_at(head, DH)
    for group, first, last in tiles.groups:
        rows = slice((first - tiles.origin) * BLOCK, (last - tiles.origin) * BLOCK)
        keys, values = key_ref[rows, lanes], value_ref[rows, lanes]
        query_rows = tokens.rows(group, head, False)
        grad_rows = tokens.rows(group, head, True)
        scores = lax.dot_general(keys, query_rows, NT, preferred_element_type=F32)
        slopes = lax.dot_general(values, grad_rows, NT, preferred_element_type=F32)
        yield group, first, last, keys, query_rows, grad_rows, scores, slopes


def piece(array, frame, position):
    return array[frame * BLOCK : (frame + 1) * BLOCK, position * BLOCK : (position + 1) * BLOCK]


def fold(stats, rate):
    tops = [jnp.where(total > 0, top, NEG) for top, total, _ in stats]
    top = functools.reduce(jnp.maximum, tops)
    gains = [jnp.exp2((t - top) * rate) for t in tops]
    total = sum(g * s[1] for g, s in zip(gains, stats))
    weighted = sum(g * s[2] for g, s in zip(gains, stats))
    return top, total, weighted


def tile_stats(bands, tiles_list, tokens, kv_refs, head, rate, kept):
    found = {}
    for tiles, (key_ref, value_ref) in zip(tiles_list, kv_refs):
        for group, first, last, _, _, _, scores, slopes in head_tiles(
            tiles, tokens, key_ref, value_ref, head
        ):
            if kept:
                kept[0][head] = scores
                kept[1][head] = slopes
            for position, t in enumerate(group):
                for f in range(first, last):
                    allowed = bands.allowed(t, f)
                    found.setdefault(t, []).append(
                        (allowed, piece(scores, f - first, position), piece(slopes, f - first, position))
                    )
    stats = {}
    for t, entries in found.items():
        shown = [s if a is None else jnp.where(a, s, NEG) for a, s, _ in entries]
        top = jnp.max(functools.reduce(jnp.maximum, shown), axis=0, keepdims=True)
        total = weighted = None
        for (allowed, _, slope), s in zip(entries, shown):
            e = jnp.exp2((s - top) * rate)
            if allowed is not None:
                e = jnp.where(allowed, e, 0.0)
            total = e if total is None else total + e
            weighted = e * slope if weighted is None else weighted + e * slope
        stats[t] = (
            top,
            jnp.sum(total, axis=0, keepdims=True),
            jnp.sum(weighted, axis=0, keepdims=True),
        )
    return stats


def read_stats(ref, head, row):
    return tuple(ref[head, row + i : row + i + 1, :] for i in range(3))


def stat_depth(own_count):
    return -(-3 * (own_count + 2) // 8) * 8


def row_stats(
    band, tiles_list, kvs, queries, grads, below, above, earlier, send, keep, rate
):
    own_count = queries.shape[0] // BLOCK
    columns = queries.shape[1]
    heads = columns // DH
    per = min(PER_LAST if send and earlier is not None and keep else PER_STATS, heads)
    depth = stat_depth(own_count)
    count = len(kvs)
    halo = any(t < 0 or t >= own_count for tiles in tiles_list for t in tiles.touched)
    shared = (queries, grads) + ((below, above) if halo else ())
    extra = [] if earlier is None else [earlier]

    def body(*refs):
        bands, refs = Bands(refs[:3], own_count), refs[3:]
        tokens = Tokens(own_count, columns, refs[: len(shared)])
        refs = refs[len(shared) :]
        kv_refs = [refs[2 * i : 2 * i + 2] for i in range(count)]
        rest = refs[2 * count :]
        out_ref = rest[len(extra)]
        kept = rest[-2:] if keep else ()
        even = lax.rem(lax.axis_index(ROWS), 2) == 0

        def step(pair, carry):
            for k in range(per):
                head = pair * per + k
                stats = tile_stats(bands, tiles_list, tokens, kv_refs, head, rate, kept)
                results = []
                blank = jnp.zeros((1, BLOCK), F32)
                for t in range(-1, own_count + 1):
                    mine = [stats[t]] if t in stats else []
                    if extra:
                        mine.append(read_stats(rest[0], head, 3 * (t + 1)))
                    if not mine:
                        mine = [(blank, blank, blank)]
                    results += mine[0] if len(mine) == 1 else fold(mine, rate)
                out_ref[head] = jnp.concatenate(
                    results + [blank] * (depth - len(results)), axis=0
                )
                if send:
                    upper, lower = [results[3 * (t + 1) : 3 * (t + 2)] for t in send]
                    for ref, flag in zip(rest[len(extra) + 1 : len(extra) + 3], (even, jnp.logical_not(even))):
                        picked = [jnp.where(flag, u, d) for u, d in zip(upper, lower)]
                        ref[head] = jnp.concatenate(picked + [blank] * 5, axis=0)
            return carry

        lax.fori_loop(0, heads // per, step, 0)

    frames = sum(kv[0].shape[0] for kv in kvs)
    flat = [array for kv in kvs for array in kv]
    shapes = [jax.ShapeDtypeStruct((heads, depth, BLOCK), F32)]
    if send:
        shapes += [jax.ShapeDtypeStruct((heads, 8, BLOCK), F32)] * 2
    if keep:
        ((group, first, end),) = tiles_list[0].groups
        shapes += [jax.ShapeDtypeStruct((heads, (end - first) * BLOCK, len(group) * BLOCK), F32)] * 2
    return call(
        body,
        [SCALARS] * 3
        + [HERE] * len(shared)
        + [HERE] * (len(flat) + len(extra)),
        [HERE] * len(shapes),
        shapes,
        [],
        8 * frames * 2 * BLOCK * columns,
        4 * frames * columns + 8 * queries.size,
    )(*band, *shared, *flat, *extra)


def term_block(buffer, at, step, key_ref, value_ref, rows, out_ref, place):
    term = lax.dot_general(
        key_ref[rows, :], buffer[at, 0, step], NT, preferred_element_type=F32
    ) + lax.dot_general(value_ref[rows, :], buffer[at, 1, step], NT, preferred_element_type=F32)
    out_ref[:, lanes_at(place, buffer.shape[3])] = term.astype(BF16)


def terms_of(buffer, begin, end, key_ref, value_ref, rows, outs, offset, before=None):
    def step(j, carry):
        if before is not None:
            before(j)
        for at, out_ref in enumerate(outs):
            term_block(buffer, at, j, key_ref, value_ref, rows, out_ref, j - begin + offset)
        return carry

    lax.fori_loop(begin, end, step, 0)
    return offset + end - begin


def gradients(
    band,
    tiles,
    kv,
    queries,
    grads,
    below,
    above,
    stats,
    swaps,
    held,
    deferred,
    kept,
    totals,
    load,
    key_weight,
    value_weight,
    rate,
    scale,
    group,
):
    own_count = queries.shape[0] // BLOCK
    columns = queries.shape[1]
    heads = columns // DH
    per = min(PER_GRADIENTS, heads)
    frames = kv[0].shape[0]
    touched = tiles.touched
    halo_touched = [t for t in touched if not 0 <= t < own_count]
    shared = (queries, grads) + ((below, above) if halo_touched else ())
    features = sum(buffer.shape[2] for buffer in held) * held[0].shape[3]
    features += held[0].shape[3] if load else 0
    later = Weights(key_weight, False, group, load) if load else None
    used = [key_weight, value_weight] if load else []
    defer = not halo_touched
    extra = [] if defer else list(deferred)
    known = [array for _, *arrays in kept for array in arrays]
    earlier = [] if totals is None else list(totals)
    base = tiles.first * BLOCK

    def body(*refs):
        bands, refs = Bands(refs[:3], own_count), refs[3:]
        tokens = Tokens(own_count, columns, refs[: len(shared)])
        refs = refs[len(shared) :]
        key_ref, value_ref, stat_ref = refs[:3]
        swap_refs, refs = refs[3 : 3 + len(swaps)], refs[3 + len(swaps) :]
        buffers, refs = refs[: len(held)], refs[len(held) :]
        both, refs = refs[: len(used)], refs[len(used) :]
        extra_refs, refs = refs[: len(extra)], refs[len(extra) :]
        known_refs, refs = refs[: len(known)], refs[len(known) + len(earlier) :]
        if load:
            *refs, held_out, sems = refs
            owners = targets(group)[1:]
            later.start(both, held_out, sems, owners)
        key_out, value_out, own_out = refs[:3]
        term_outs = refs[3 : 2 + group]
        halo_outs = refs[2 + group :]
        even = lax.rem(lax.axis_index(ROWS), 2) == 0

        def one(head):
            lanes = lanes_at(head, DH)
            rows = {}
            for t in touched:
                parts = [read_stats(stat_ref, head, 3 * (t + 1))]
                even_ref, odd_ref = swap_refs[:2] if 0 <= t < own_count else swap_refs[2:]
                first, second = read_stats(even_ref, head, 0), read_stats(odd_ref, head, 0)
                if t <= 0:
                    parts.append([jnp.where(even, b, a) for a, b in zip(first, second)])
                if t >= own_count - 1:
                    parts.append([jnp.where(even, a, b) for a, b in zip(first, second)])
                top, total, weighted = fold(parts, rate)
                rows[t] = (top * rate + jnp.log2(total), weighted / total)
            key_sum = [None] * (tiles.last - tiles.first)
            value_sum = [None] * (tiles.last - tiles.first)
            query_sum = {}
            if extra:
                query_part = lax.dot_general(
                    extra_refs[1][head], extra_refs[0][:, lanes], TN, preferred_element_type=F32
                )
                for t in range(own_count):
                    query_sum[t] = query_part[t * BLOCK : (t + 1) * BLOCK]
            for group_tokens, first, last in tiles.groups:
                cut = slice((first - tiles.origin) * BLOCK, (last - tiles.origin) * BLOCK)
                query_rows = tokens.rows(group_tokens, head, False)
                grad_rows = tokens.rows(group_tokens, head, True)
                if known:
                    scores = [known_refs[2 * i][head] for i in range(len(kept))]
                    slopes = [known_refs[2 * i + 1][head] for i in range(len(kept))]
                    scores, slopes = jnp.concatenate(scores), jnp.concatenate(slopes)
                else:
                    keys, values = key_ref[cut, lanes], value_ref[cut, lanes]
                    scores = lax.dot_general(keys, query_rows, NT, preferred_element_type=F32)
                    slopes = lax.dot_general(values, grad_rows, NT, preferred_element_type=F32)
                low, slope_low = [], []
                for f in range(first, last):
                    low_row, slope_row = [], []
                    for position, t in enumerate(group_tokens):
                        level, delta = rows[t]
                        p = jnp.exp2(piece(scores, f - first, position) * rate - level)
                        d = p * (piece(slopes, f - first, position) - delta) * scale
                        allowed = bands.allowed(t, f)
                        if allowed is not None:
                            p = jnp.where(allowed, p, 0.0)
                            d = jnp.where(allowed, d, 0.0)
                        low_row.append(p.astype(BF16))
                        slope_row.append(d.astype(BF16))
                    low.append(jnp.concatenate(low_row, axis=1))
                    slope_low.append(jnp.concatenate(slope_row, axis=1))
                low = jnp.concatenate(low, axis=0)
                slope_low = jnp.concatenate(slope_low, axis=0)
                key_part = jnp.dot(slope_low, query_rows, preferred_element_type=F32)
                value_part = jnp.dot(low, grad_rows, preferred_element_type=F32)
                if defer:
                    own_out[head] = slope_low
                else:
                    query_part = lax.dot_general(slope_low, keys, TN, preferred_element_type=F32)
                    for position, t in enumerate(group_tokens):
                        part = query_part[position * BLOCK : (position + 1) * BLOCK]
                        query_sum[t] = query_sum[t] + part if t in query_sum else part
                for f in range(first, last):
                    at, cut = f - tiles.first, slice((f - first) * BLOCK, (f - first + 1) * BLOCK)
                    for sums, part in ((key_sum, key_part), (value_sum, value_part)):
                        sums[at] = part[cut] if sums[at] is None else sums[at] + part[cut]
            for at in range(tiles.last - tiles.first):
                cut = slice(base + at * BLOCK, base + (at + 1) * BLOCK)
                key_out[cut, lanes] = key_sum[at].astype(BF16)
                value_out[cut, lanes] = value_sum[at].astype(BF16)
            if not defer:
                for t in range(own_count):
                    part = query_sum[t] if t in query_sum else jnp.zeros((BLOCK, DH), F32)
                    own_out[t * BLOCK : (t + 1) * BLOCK, lanes] = part
                for out_ref, t in zip(halo_outs, halo_touched):
                    out_ref[:, lanes] = query_sum[t]

        def step(pair, carry):
            for k in range(per):
                one(pair * per + k)
            return carry

        lax.fori_loop(0, heads // per, step, 0)

        place, rows = 0, slice(base, base + frames)
        for buffer in buffers:
            place = terms_of(buffer, 0, buffer.shape[2], key_out, value_out, rows, term_outs, place)
        if load:
            later.wait(both, held_out, sems, owners, 0)
            terms_of(held_out, 0, 1, key_out, value_out, rows, term_outs, place)
            for j in range(1, later.steps):
                later.wait(both, held_out, sems, owners, j)

    shapes = (
        [jax.ShapeDtypeStruct((RATIO * own_count * BLOCK, columns), BF16)] * 2
        + [
            jax.ShapeDtypeStruct((heads, frames, own_count * BLOCK), BF16)
            if defer
            else jax.ShapeDtypeStruct((own_count * BLOCK, columns), F32)
        ]
        + [jax.ShapeDtypeStruct((frames, features), BF16)] * (group - 1)
        + [jax.ShapeDtypeStruct((BLOCK, columns), F32)] * len(halo_touched)
        + ([jax.ShapeDtypeStruct(later.buffer_shape(group - 1), BF16)] if load else [])
    )
    out = call(
        body,
        [SCALARS] * 3
        + [HERE] * (len(shared) + 3 + len(swaps))
        + [HERE] * len(held)
        + [ANYWHERE] * len(used)
        + [HERE] * (len(extra) + len(known) + len(earlier)),
        [HERE] * len(shapes),
        shapes,
        [later.semaphores(group - 1)] if load else [],
        20 * frames * 2 * BLOCK * columns + 4 * frames * columns * features * (group - 1),
        8 * frames * columns,
        {
            6 + len(held) + len(used) + len(swaps) + len(shared) + len(extra) + len(known) + i: i
            for i in range(len(earlier))
        },
    )(*band, *shared, *kv, stats, *swaps, *held, *used, *extra, *known, *earlier)
    halo = dict(zip(halo_touched, out[2 + group :]))
    return out[:2], out[2], out[3 : 2 + group], halo, out[-1] if load else None


def more_terms(totals, first, frames, held, span, key_weight, value_weight, group):
    columns = totals[0].shape[1]
    later = Weights(key_weight, False, group, span)
    features = (held.shape[2] - 1 + later.steps) * later.step
    shapes = [jax.ShapeDtypeStruct((frames, features), BF16)] * (group - 1)
    shapes.append(jax.ShapeDtypeStruct(later.buffer_shape(group - 1), BF16))

    def body(key_ref, value_ref, buffer, key_weight_ref, value_weight_ref, *refs):
        *outs, held_out, sems = refs
        both, owners = (key_weight_ref, value_weight_ref), targets(group)[1:]
        later.start(both, held_out, sems, owners)
        rows = slice(first, first + frames)

        def before(j):
            later.wait(both, held_out, sems, owners, j)

        place = terms_of(buffer, 1, held.shape[2], key_ref, value_ref, rows, outs, 0)
        terms_of(held_out, 0, later.steps, key_ref, value_ref, rows, outs, place, before)

    return call(
        body,
        [HERE] * 3 + [ANYWHERE] * 2,
        [HERE] * len(shapes),
        shapes,
        [later.semaphores(group - 1)],
        4 * frames * columns * features * (group - 1),
        4 * frames * columns,
    )(*totals, held, key_weight, value_weight)


def own_terms(totals, key_weight, value_weight, group):
    rows, columns = totals[0].shape
    weights = Weights(key_weight, False, group)

    def body(key_grad_ref, value_grad_ref, key_ref, value_ref, out_ref, buffer, sems):
        both = key_ref, value_ref
        owners = targets(group)[:1]
        weights.start(both, buffer, sems, owners, WINDOW)

        def step(j, carry):
            weights.advance(both, buffer, sems, owners, j)
            term_block(buffer, 0, j, key_grad_ref, value_grad_ref, slice(0, rows), out_ref, j)
            return carry

        lax.fori_loop(0, weights.steps, step, 0)

    return call(
        body,
        [HERE] * 2 + [ANYWHERE] * 2,
        HERE,
        jax.ShapeDtypeStruct((rows, weights.features), BF16),
        [weights.scratch(1), weights.semaphores(1)],
        4 * rows * columns * weights.features,
        4 * columns * weights.features,
    )(*totals, key_weight, value_weight)


def finish_queries(low, high, from_below, from_above):
    rows, columns = low.shape
    tall = BLOCK
    steps = rows // tall

    def body(low_ref, high_ref, below_ref, above_ref, out_ref, buffer, sems):
        copies = []
        for i in range(steps):
            cut = slice(i * tall, (i + 1) * tall)
            total = low_ref[cut, :] + high_ref[cut, :]
            if i == 0:
                total = total + below_ref[...]
            if i == steps - 1:
                total = total + above_ref[...]
            buffer[i] = total.astype(BF16)
            copies.append(pltpu.make_async_copy(buffer.at[i], out_ref.at[pl.ds(i * tall, tall), :], sems.at[i]))
            copies[-1].start()
        for copy in copies:
            copy.wait()

    return call(
        body,
        [HERE] * 4,
        ANYWHERE,
        pltpu.HBM((rows, columns), BF16),
        [pltpu.VMEM((steps, tall, columns), BF16), pltpu.SemaphoreType.DMA((steps,))],
        4 * rows * columns,
        12 * rows * columns,
    )(low, high, from_below, from_above)


def add_rows(target, own, arrived):
    features = own.shape[1]
    tall = BLOCK // 2
    flat = [array for _, turns in arrived for turn in turns for array in turn]
    sizes = [turns[0][0].shape[0] // tall for _, turns in arrived]

    def body(own_ref, *refs):
        out_ref, buffer, sems = refs[-3:]
        copies = []
        at = slot = 0
        for (first, turns), steps in zip(arrived, sizes):
            terms = []
            for turn in turns:
                terms.append(refs[at : at + len(turn)])
                at += len(turn)
            for i in range(steps):
                rows = slice(first + i * tall, first + (i + 1) * tall)
                left = 0
                for side in range(len(turns[0])):
                    right = left + terms[0][side].shape[1]
                    value = own_ref[rows, left:right].astype(F32)
                    for turn in terms:
                        value = value + turn[side][i * tall : (i + 1) * tall, :].astype(F32)
                    buffer[slot, :, left:right] = value.astype(BF16)
                    left = right
                copy = pltpu.make_async_copy(
                    buffer.at[slot], out_ref.at[pl.ds(first + i * tall, tall), :], sems.at[slot]
                )
                copy.start()
                copies.append(copy)
                slot += 1
        for copy in copies:
            copy.wait()

    extra = [] if target is None else [target]
    slots = sum(sizes)
    return call(
        body,
        [HERE] * (1 + len(flat)) + [ANYWHERE] * len(extra),
        ANYWHERE,
        pltpu.HBM(own.shape, own.dtype),
        [pltpu.VMEM((slots, tall, features), BF16), pltpu.SemaphoreType.DMA((slots,))],
        slots * tall * features,
        6 * slots * tall * features,
        {1 + len(flat): 0} if extra else None,
    )(own, *flat, *extra)


def shifted(value, steps):
    count = lax.axis_size(ROWS)
    first, last = (max(0, -steps), min(count, count - steps))
    return lax.ppermute(value, ROWS, [(source, source + steps) for source in range(first, last)])


def swapped(value, first):
    pairs = []
    for at in range(first, lax.axis_size(ROWS) - 1, 2):
        pairs += [(at, at + 1), (at + 1, at)]
    return lax.ppermute(value, ROWS, pairs)


def on_device(encoder_states, key_weight, value_weight, queries, out_grad, band_blocks):
    frames = encoder_states.shape[0]
    tokens = queries.shape[0]
    own_count = tokens // BLOCK
    frame_blocks = frames // BLOCK
    scale = DH ** (-0.5)
    rate = scale * math.log2(math.e)
    group = lax.axis_size("tensor")
    edge = HALO_BLK
    middle = frame_blocks // 2
    cuts = [(0, edge), (frame_blocks - edge, frame_blocks), (edge, middle), (middle, frame_blocks - edge)]
    row_cuts = [(first * BLOCK, last * BLOCK) for first, last in cuts]
    turns = [[(i, (i + k) % group) for i in range(group)] for k in range(1, group)]

    key_weight, value_weight = [
        pltpu.with_memory_space_constraint(w, pltpu.HBM) for w in (key_weight, value_weight)
    ]
    depth = encoder_states.shape[1]
    split = max(depth // 2 // BLOCK, 1) * BLOCK
    parts = [(first, last, 0, depth) for first, last in row_cuts[:-1]]
    parts += [(*row_cuts[-1], 0, split), (*row_cuts[-1], split, depth)]
    arrived = []
    for rows in take_parts(encoder_states, parts[:1]) + take_parts(encoder_states, parts[1:]):
        arrived.append([lax.ppermute(rows, "tensor", turn) for turn in turns])

    edge_up, edge_down = take_edges(queries, out_grad)
    below = shifted(edge_up, 1)
    above = shifted(edge_down, -1)
    band = (shifted(band_blocks, 1), band_blocks, shifted(band_blocks, -1))

    partial = project_own(encoder_states, key_weight, value_weight, row_cuts, group)

    def rest(i, part, held, **place):
        return project_rest(part, arrived[i], key_weight, value_weight, held, group, **place)

    def statistics(*where, **what):
        return row_stats(band, *where, queries, out_grad, below, above, *what.values(), rate)

    def exchange(arrays):
        return tuple(swapped(array, first) for first, array in enumerate(arrays))

    low_tiles, high_tiles = [Tiles(own_count, first, last, True) for first, last in cuts[:2]]
    inner = [Tiles(own_count, first, last, False, edge) for first, last in cuts[2:]]
    inner_tiles = Tiles(own_count, edge, frame_blocks - edge, False)
    low_kv, held = rest(0, partial[0], None)
    (stats,) = statistics([low_tiles], [low_kv], earlier=None, send=None, keep=False)
    high_kv, _ = rest(1, partial[1], held)
    stats, *outer = statistics([high_tiles], [high_kv], earlier=stats, send=(own_count, -1), keep=False)
    early = exchange(outer)
    height = (frame_blocks - 2 * edge) * BLOCK
    kv, _ = rest(2, partial[2], held, height=height)
    stats, *first_kept = statistics(inner[:1], [kv], earlier=stats, send=None, keep=True)
    kv, stats = lax.optimization_barrier((kv, stats))
    spans = away_spans(key_weight, group)
    part, first_held = rest(3, partial[3], held, final=False, away=spans[0])
    inner_kv, _ = rest(
        4, part, held, left=split, base=(middle - edge) * BLOCK, height=height, into=kv
    )
    stats, first_own, second_own, *second_kept = statistics(
        inner[1:], [inner_kv], earlier=stats, send=(own_count - 1, 0), keep=True
    )
    late = exchange((first_own, second_own))
    kept = [(edge, *first_kept), (middle, *second_kept)]

    chunks = [(inner_tiles, inner_kv), (low_tiles, low_kv), (high_tiles, high_kv)]
    shared = (queries, out_grad, below, above, stats)
    out, sent = [], []
    totals = None
    deferred = ()
    away = [first_held]
    for i, (tiles, kv) in enumerate(chunks):
        out.append(
            gradients(
                band,
                tiles,
                kv,
                *shared,
                early + late if i else early,
                away,
                deferred,
                () if i else kept,
                totals,
                None if i else spans[1],
                key_weight,
                value_weight,
                rate,
                scale,
                group,
            )
        )
        totals = out[i][0]
        deferred = (inner_kv[0], out[0][1]) if i == 1 else ()
        sent.append([[lax.ppermute(term, "tensor", turn)] for term, turn in zip(out[i][2], turns)])
        if i == 0:
            *more, last_held = more_terms(
                totals,
                tiles.first * BLOCK,
                kv[0].shape[0],
                out[0][4],
                spans[2],
                key_weight,
                value_weight,
                group,
            )
            away = [first_held, out[0][4], last_held]
            for turn_sent, term, turn in zip(sent[0], more, turns):
                turn_sent.append(lax.ppermute(term, "tensor", turn))

    from_below = shifted(out[2][3][own_count], 1)
    from_above = shifted(out[1][3][-1], -1)
    own = own_terms(totals, key_weight, value_weight, group)
    query_grad = finish_queries(out[1][1], out[2][1], from_below, from_above)

    back = [(tiles.first * BLOCK, turns_sent) for (tiles, _), turns_sent in zip(chunks, sent)]
    encoder_grad = add_rows(None, own, back[:-1])
    encoder_grad = add_rows(encoder_grad, own, back[-1:])
    return (query_grad, encoder_grad)


def solution(mesh):
    return jax.shard_map(
        on_device,
        mesh=mesh,
        in_specs=(
            P(ROWS, "tensor"),
            P(None, "tensor"),
            P(None, "tensor"),
            P(ROWS, "tensor"),
            P(ROWS, "tensor"),
            P(ROWS, None),
        ),
        out_specs=(P(ROWS, "tensor"), P(ROWS, "tensor")),
        check_vma=False,
    )
```
